32 devices in a mesh: space: 8 (over y, x, core), mp: 4 (over z).
Axes of the slice: x: 2, y: 2, z: 4, core: 2. Of those that a mesh axis runs over, the one named last changes fastest.
Arguments:
- tokens: bfloat16 [12288, 1024], P('space')
- norm_gain: float32 [1024], replicated, may hold values from 0.5 to 1.5
- w_qkv: bfloat16 [1024, 4, 192], P(None, 'mp')
- w_out: bfloat16 [256, 1024], replicated, may hold values from -0.75 to 0.75
- head_scale: float32 [4], P('mp'), may hold values from 8 to 400
- cycle_to_nested: int32 [12288], P('space'), may hold values from 0 to 12287, as said below
- neighbours: int32 [96, 9], P('space'), may hold values from -1 to 95, as said below
Outputs:
- mixed: bfloat16 [12288, 1024], P(('space', 'mp'))
The draws below stay inside these ranges and needn't reach their ends.
Inputs may be any that keep to these rules, and one draw needn't show every extreme that they name: `cycle_to_nested`: A permutation of the tokens; the cycle rows of each index of space hold exactly 192 of the nested places of each index of space, the block of 1536 places of that index. `neighbours`: slot 0 names the block itself; the other slots name distinct other blocks at most 6 places away in block order, counted around the end of the order; only slots 7 and 8 may be -1.
All inputs are finite; a program needn't handle non-finite values.
Results may differ from the reference program's by a relative error of at most 0.012.
The reference program's roundings to bfloat16 on the way count: a program that leaves them out, or rounds other values in their place, can miss the bound.
Values may be sent and summed in bfloat16 or wider, within the bound.
No kernel may reach another device: no remote copies, remote signals or barrier semaphores. Data moves between devices by JAX's collectives and lax.ppermute only.
A program may use at most 64 MiB of HBM per device.

```python
import math
import jax
import jax.numpy as jnp
from jax import lax

D = 1024
HD = 64
BLOCK = 128
NEIGH = 9
REACH = 6
HEADS = 4
TOK_DEV = 1536
TOKENS = 12288
NBLK = 96


def draw_tokens(key, part):
    gathered_key_rows = jax.random.split(jax.random.fold_in(key, 1), 2)
    base = jax.random.normal(gathered_key_rows[0], (TOKENS, D), jnp.float32)
    row_scale = jnp.exp(jax.random.uniform(gathered_key_rows[1], (TOKENS, 1), jnp.float32, 0.0, math.log(10.0)))
    values = base * row_scale
    return values.astype(jnp.bfloat16)


def draw_w_qkv(key, part):
    gathered_key_rows = jax.random.split(jax.random.fold_in(key, 2), 3)
    spread = D ** (-0.5)
    w_query = jax.random.normal(gathered_key_rows[0], (D, HEADS, HD), jnp.float32) * spread
    w_value = jax.random.normal(gathered_key_rows[2], (D, HEADS, HD), jnp.float32) * spread
    noise = jax.random.normal(gathered_key_rows[1], (D, HEADS, HD), jnp.float32) * spread
    w_key = noise
    return jnp.concatenate([w_query, w_key, w_value], axis=2).astype(jnp.bfloat16)


def draw_head_scale(key, part):
    sample = jax.random.uniform(jax.random.fold_in(key, 3), (HEADS,), jnp.float32)
    lower, upper = (math.log(8.0), math.log(40.0))
    return jnp.exp(lower + (upper - lower) * sample)


def draw_cycle_to_nested(key, part):
    device_count = TOKENS // TOK_DEV
    group_rows = TOK_DEV // device_count
    gathered_key_rows = jax.random.split(jax.random.fold_in(key, 4), 2)
    first_keys = jax.random.split(gathered_key_rows[0], device_count)
    second_keys = jax.random.split(gathered_key_rows[1], device_count)
    source_perm = jax.vmap(lambda one_key: jax.random.permutation(one_key, TOK_DEV))(first_keys)
    target_perm = jax.vmap(lambda one_key: jax.random.permutation(one_key, TOK_DEV))(second_keys)
    source_ids = jnp.arange(device_count, dtype=jnp.int32)[:, None]
    target_dev = source_perm // group_rows
    within = source_perm % group_rows
    place = target_perm[target_dev, source_ids * group_rows + within]
    return (target_dev * TOK_DEV + place).reshape(-1).astype(jnp.int32)


def draw_neighbours(key, part):
    gathered_key_rows = jax.random.split(jax.random.fold_in(key, 5), 2)
    offsets = jnp.concatenate([jnp.arange(-REACH, 0, dtype=jnp.int32), jnp.arange(1, REACH + 1, dtype=jnp.int32)])
    ranking = jax.random.randint(gathered_key_rows[0], (NBLK, 2 * REACH), 0, 1 << 20) * (2 * REACH) + jnp.arange(2 * REACH, dtype=jnp.int32)[None, :]
    picked = jnp.argsort(ranking, axis=1)[:, :NEIGH - 1]
    chosen = offsets[picked]
    block_ids = jnp.arange(NBLK, dtype=jnp.int32)[:, None]
    others = jnp.mod(block_ids + chosen, NBLK)
    full = jnp.concatenate([block_ids, others], axis=1)
    corner = (jax.random.randint(gathered_key_rows[1], (NBLK,), 0, 16) == 0) | (jnp.arange(NBLK) == 0)
    dropped = corner[:, None] & (jnp.arange(NEIGH)[None, :] >= NEIGH - 2)
    return jnp.where(dropped, -1, full).astype(jnp.int32)


def centred(key, shape, deviation, limit, kind=jnp.bfloat16):
    values = jax.random.normal(key, shape, jnp.float32) * deviation
    return jnp.minimum(jnp.maximum(values, -limit), limit).astype(kind)


def setup_inputs(seed: int = 0) -> dict:
    streams_of = jax.random.split(jax.random.key(seed), 8)
    return {
        "tokens": draw_tokens(jax.random.fold_in(streams_of[7], 71), 0),
        "norm_gain": jnp.clip(1.0 + 0.1 * jax.random.normal(streams_of[1], (D,), jnp.float32), 0.5, 1.5),
        "w_qkv": draw_w_qkv(jax.random.fold_in(streams_of[7], 71), 0),
        "w_out": centred(streams_of[3], (HEADS * HD, D), HD ** -0.5, 0.75),
        "head_scale": draw_head_scale(jax.random.fold_in(streams_of[7], 71), 0),
        "cycle_to_nested": draw_cycle_to_nested(jax.random.fold_in(streams_of[7], 71), 0),
        "neighbours": draw_neighbours(jax.random.fold_in(streams_of[7], 71), 0),
    }


def norm_rows(tokens, norm_gain):
    values = tokens.astype(jnp.float32)
    mean_square = lax.optimization_barrier(jnp.mean(values * values, axis=1, keepdims=True))
    return (values * lax.rsqrt(mean_square + 1e-05) * norm_gain).astype(jnp.bfloat16)

def project_head(normed, weight_head, scale_value, head_dim):
    projected = jnp.dot(normed, weight_head, preferred_element_type=jnp.float32)
    query_rows = projected[:, :head_dim]
    key_raw = projected[:, head_dim:2 * head_dim]
    values = projected[:, 2 * head_dim:]
    query_rows = query_rows * (scale_value * lax.rsqrt(lax.optimization_barrier(jnp.sum(query_rows * query_rows, axis=1, keepdims=True)) + 1e-06))
    key_raw = key_raw * lax.rsqrt(lax.optimization_barrier(jnp.sum(key_raw * key_raw, axis=1, keepdims=True)) + 1e-06)
    return jnp.concatenate([query_rows, key_raw, values], axis=1).astype(jnp.bfloat16)

def attend_blocks(query_rows, kv_blocks, positions, present, head_dim):
    block_rows = query_rows.shape[1]
    gathered = kv_blocks[positions]
    batch_blocks = gathered.shape[0]
    gathered_key_rows = gathered[..., :head_dim].reshape(batch_blocks, -1, head_dim)
    gathered_value_rows = gathered[..., head_dim:].reshape(batch_blocks, -1, head_dim)
    score_matrix = jnp.einsum('ltv,lpv->ltp', query_rows.astype(jnp.float32), gathered_key_rows.astype(jnp.float32))
    key_mask = jnp.repeat(present, block_rows, axis=1)[:, None, :]
    score_matrix = jnp.where(key_mask, score_matrix, -1e+30)
    row_max = lax.optimization_barrier(jnp.max(score_matrix, axis=2, keepdims=True))
    exponent = jnp.exp(score_matrix - row_max)
    row_total = lax.optimization_barrier(jnp.sum(exponent, axis=2, keepdims=True))
    attention_weight = exponent.astype(jnp.bfloat16)
    weighted_sum = jnp.einsum('uct,uth->uch', attention_weight.astype(jnp.float32), gathered_value_rows.astype(jnp.float32))
    return (weighted_sum / row_total).astype(jnp.bfloat16)

def reference(tokens, norm_gain, w_qkv, w_out, head_scale, cycle_to_nested, neighbours):
    normed = norm_rows(tokens, norm_gain)
    present = neighbours >= 0
    positions = jnp.where(present, neighbours, 0).astype(jnp.int32)

    def one_head(head):
        weight_head = lax.dynamic_index_in_dim(w_qkv, head, 1, keepdims=False)
        packed = project_head(normed, weight_head, head_scale[head], HD)
        nested_ordering = jnp.zeros_like(packed).at[cycle_to_nested].set(packed)
        query_rows = nested_ordering[:, :HD].reshape(NBLK, BLOCK, HD)
        kv_blocks = nested_ordering[:, HD:].reshape(NBLK, BLOCK, 2 * HD)

        def one_block(item):
            query_block, block_pos, block_present = item
            return attend_blocks(query_block[None], kv_blocks, block_pos[None], block_present[None], HD)[0]
        outputs = lax.map(one_block, (query_rows, positions, present), batch_size=64)
        return outputs.reshape(TOKENS, HD)
    heads_out = lax.map(one_head, jnp.arange(HEADS, dtype=jnp.int32))
    attn = jnp.transpose(heads_out, (1, 0, 2)).reshape(TOKENS, HEADS * HD)
    return jnp.dot(attn, w_out, preferred_element_type=jnp.float32).astype(jnp.bfloat16)
```

```python
import functools

import jax
import jax.numpy as jnp
from jax import lax
from jax.experimental import pallas as pl
from jax.experimental.pallas import tpu as pltpu
from jax.sharding import PartitionSpec as P

BLOCK = 128
REACH = 6
LANES = 128
TILE = 256
F32 = jnp.float32
BF16 = jnp.bfloat16


def dot(a, b):
    return jnp.dot(a, b, preferred_element_type=F32)


def dot_nt(a, b):
    return lax.dot_general(a, b, (((1,), (1,)), ((), ())), preferred_element_type=F32)


def iota(shape, dim):
    return lax.broadcasted_iota(jnp.int32, shape, dim)


def send_kernel(space, tok, tokens_hbm, gain_ref, w_ref, scale_ref, slots_ref, out_ref,
                tok_buf, packed_buf, pos_buf, sems):
    tiles = tok // TILE
    group = tok // space
    head = w_ref.shape[1] // 3
    copies = [
        pltpu.make_async_copy(
            tokens_hbm.at[pl.ds(i * TILE, TILE), :], tok_buf.at[i], sems.at[i]
        )
        for i in range(tiles)
    ]
    for copy in copies:
        copy.start()

    slots = slots_ref[...]
    rows = slots.shape[0]
    masks = [((slots >= d * tok) & (slots < (d + 1) * tok)) for d in range(space)]
    ones = [m.astype(F32) for m in masks]
    stacked = jnp.concatenate(ones, axis=0).astype(BF16)
    total_rows = rows * space
    earlier = (iota((LANES, LANES), 0) < iota((LANES, LANES), 1)).astype(F32).astype(BF16)
    in_row = dot(stacked, earlier)
    row_total = dot(stacked, jnp.ones((LANES, LANES), BF16)).astype(BF16)
    left, right = iota((total_rows, total_rows), 0), iota((total_rows, total_rows), 1)
    above = ((left // rows == right // rows) & (right < left)).astype(F32).astype(BF16)
    rank = in_row + dot(above, row_total)
    pos = jnp.full((rows, LANES), -1.0, F32)
    place = slots
    for d in range(space):
        pos = jnp.where(masks[d], rank[d * rows : (d + 1) * rows] + float(d * group), pos)
        place = jnp.where(masks[d], slots - d * tok, place)
    pos_buf[...] = pos.astype(jnp.int32)
    high = (place >> 7).astype(F32)
    low = (place & 127).astype(F32)
    columns = jnp.concatenate(
        [high, low, jnp.zeros((LANES - 2 * rows, LANES), F32)], axis=0
    ).T

    weights = w_ref[...].astype(F32)
    weights = jnp.concatenate(
        [weights[:, head:], weights[:, :head], jnp.zeros((weights.shape[0], TILE - 3 * head), F32)],
        axis=1,
    ).astype(BF16)
    gain = gain_ref[...]
    scale = scale_ref[0]
    lane = iota((TILE, LANES), 1)
    for i in range(tiles):
        copies[i].wait()
        values = tok_buf[i].astype(F32)
        mean_square = jnp.mean(values * values, axis=1, keepdims=True)
        normed = (values * lax.rsqrt(mean_square + 1e-05) * gain).astype(BF16)
        projected = dot(normed, weights)
        key_value = projected[:, :LANES]
        query = projected[:, LANES:]
        squares = jnp.where(lane < head, key_value * key_value, 0.0)
        key_factor = lax.rsqrt(jnp.sum(squares, axis=1, keepdims=True) + 1e-06)
        key_value = jnp.where(lane < head, key_value * key_factor, key_value)
        query = query * (
            scale * lax.rsqrt(jnp.sum(query * query, axis=1, keepdims=True) + 1e-06)
        )
        first = i * (TILE // LANES)
        for part in range(TILE // LANES):
            r = first + part
            span = slice(part * LANES, (part + 1) * LANES)
            marked = jnp.where(
                lane[span] == head,
                columns[:, r : r + 1],
                jnp.where(lane[span] == head + 1, columns[:, rows + r : rows + r + 1], query[span]),
            )
            packed_buf[r * LANES : (r + 1) * LANES, LANES:] = marked.astype(BF16)
        packed_buf[i * TILE : (i + 1) * TILE, :LANES] = key_value.astype(BF16)

    step = 384

    def permute(n, carry):
        start = pl.multiple_of(n * step, step)
        wanted = iota((step, LANES), 0) + start
        chosen = jnp.concatenate(
            [
                (wanted == pos_buf[r : r + 1, :]).astype(F32).astype(BF16)
                for r in range(tok // LANES)
            ],
            axis=1,
        )
        out_ref[pl.ds(start, step), :] = dot(chosen, packed_buf[...]).astype(BF16)
        return carry

    lax.fori_loop(0, tok // step, permute, 0)


def nest_kernel(head, got_ref, kv_ref, q_ref):
    tok = got_ref.shape[0]
    lane = iota((8, LANES), 1)
    row = iota((8, LANES), 0)
    pick = (lane == row + head).astype(F32).astype(BF16)
    parts = dot_nt(pick, got_ref[:, LANES:])
    slots = (parts[0:1] * float(BLOCK) + parts[1:2]).astype(jnp.int32)
    step = 384
    keep = iota((step, LANES), 1) < head

    def place(n, carry):
        start = pl.multiple_of(n * step, step)
        chosen = (iota((step, tok), 0) + start == slots).astype(F32).astype(BF16)
        nested = dot(chosen, got_ref[...])
        kv_ref[pl.ds(start, step), :] = nested[:, :LANES].astype(BF16)
        q_ref[pl.ds(start, step), :] = jnp.where(keep, nested[:, LANES:], 0.0).astype(BF16)
        return carry

    lax.fori_loop(0, tok // step, place, 0)


def attend_kernel(head, blocks, region_blocks, all_blocks, target_ref, base_ref, near_ref,
                  q_ref, kv_ref, out_ref):
    half = blocks * BLOCK // 2
    outputs = []
    for i in range(blocks):
        b = target_ref[0] * blocks + i
        tiles, biases = [], []
        for s in range(9):
            near = near_ref[b, s]
            apart = near - base_ref[0]
            apart = jnp.where(apart >= all_blocks // 2, apart - all_blocks, apart)
            apart = jnp.where(apart < -(all_blocks // 2), apart + all_blocks, apart)
            at = jnp.where(near >= 0, apart + REACH, b + REACH)
            at = jnp.clip(at, 0, region_blocks + 2 * REACH - 1)
            tiles.append(kv_ref[pl.ds(pl.multiple_of(at * BLOCK, BLOCK), BLOCK), :])
            biases.append(near >= 0)
        keys = jnp.concatenate(tiles, axis=0)
        query = q_ref[pl.ds(pl.multiple_of(b * BLOCK, BLOCK), BLOCK), :]
        scores = dot_nt(query, keys)
        parts = [scores[:, s * BLOCK : (s + 1) * BLOCK] for s in range(9)]
        for s in (7, 8):
            parts[s] = jnp.where(biases[s], parts[s], -1e30)
        top = functools.reduce(jnp.maximum, parts)
        top = jnp.max(top, axis=1, keepdims=True)
        exps = [jnp.exp(part - top) for part in parts]
        total = jnp.sum(functools.reduce(jnp.add, exps), axis=1, keepdims=True)
        weights = jnp.concatenate([e.astype(BF16) for e in exps], axis=1)
        outputs.append(dot(weights, keys) / total)
    rows = jnp.concatenate(outputs, axis=0)
    lane = iota((half, LANES), 1)
    out_ref[...] = jnp.where(
        lane < head, pltpu.roll(rows[:half], head, 1), rows[half:]
    ).astype(BF16)


def mix_kernel(mp, head, heads_ref, *refs):
    parts, w_ref, out_ref, buf = refs[:mp], refs[mp], refs[mp + 1], refs[mp + 2]
    half = parts[0].shape[0]
    for k in range(mp):
        buf[heads_ref[k]] = parts[k][...]
    lane = iota((half, LANES), 1)
    upper, lower = [], []
    for pair in range(mp // 2):
        a = buf[2 * pair].astype(F32)
        b = buf[2 * pair + 1].astype(F32)
        upper.append(jnp.where(lane < head, a, pltpu.roll(b, head, 1)).astype(BF16))
        lower.append(jnp.where(lane < head, pltpu.roll(a, head, 1), b).astype(BF16))
    weights = w_ref[...]
    out_ref[:half, :] = dot(jnp.concatenate(upper, axis=1), weights).astype(BF16)
    out_ref[half:, :] = dot(jnp.concatenate(lower, axis=1), weights).astype(BF16)


VMEM = pl.BlockSpec(memory_space=pltpu.VMEM)
SMEM = pl.BlockSpec(memory_space=pltpu.SMEM)
HBM = pl.BlockSpec(memory_space=pl.ANY)


def params(mib):
    return pltpu.CompilerParams(vmem_limit_bytes=mib << 20)


def per_device(tokens, norm_gain, w_qkv, w_out, head_scale, cycle_to_nested, neighbours):
    tok, width = tokens.shape
    space, mp = lax.axis_size("space"), lax.axis_size("mp")
    head = w_qkv.shape[2] // 3
    region = lax.axis_index("space")
    part = lax.axis_index("mp")
    row_count = -(-tok // (8 * LANES)) * 8
    slots = cycle_to_nested.reshape(tok // LANES, LANES)
    slots = jnp.pad(slots, ((0, row_count - tok // LANES), (0, 0)), constant_values=-1)
    sorted_rows = pl.pallas_call(
        functools.partial(send_kernel, space, tok),
        out_shape=jax.ShapeDtypeStruct((tok, TILE), BF16),
        in_specs=[HBM, VMEM, VMEM, SMEM, VMEM],
        out_specs=VMEM,
        scratch_shapes=[
            pltpu.VMEM((tok // TILE, TILE, width), BF16),
            pltpu.VMEM((tok, TILE), BF16),
            pltpu.VMEM((row_count, LANES), jnp.int32),
            pltpu.SemaphoreType.DMA((tok // TILE,)),
        ],
        compiler_params=params(24),
        name="send",
    )(tokens, norm_gain.reshape(1, width), w_qkv.reshape(width, 3 * head), head_scale, slots)
    got = lax.all_to_all(
        sorted_rows.reshape(space, tok // space, TILE), "space", 0, 0, tiled=True
    ).reshape(tok, TILE)
    kv, query = pl.pallas_call(
        functools.partial(nest_kernel, head),
        out_shape=(jax.ShapeDtypeStruct((tok, LANES), BF16),) * 2,
        in_specs=[VMEM],
        out_specs=(VMEM, VMEM),
        compiler_params=params(16),
        name="nest",
    )(got)
    edge = REACH * BLOCK
    up = [(i, (i + 1) % space) for i in range(space)]
    down = [(j, i) for i, j in up]
    before = lax.ppermute(kv[tok - edge :], "space", up)
    after = lax.ppermute(kv[:edge], "space", down)
    extended = jnp.concatenate([before, kv, after], axis=0)
    region_blocks = tok // BLOCK
    blocks = region_blocks // mp
    base = (region * region_blocks).reshape(1)
    pairs = mp & (mp - 1) == 0
    received, heads = [], []
    for k in range(mp - 1, -1, -1):
        target = (part ^ k) if pairs else (part + k) % mp
        source = (part ^ k) if pairs else (part - k) % mp
        chunk = pl.pallas_call(
            functools.partial(attend_kernel, head, blocks, region_blocks, region_blocks * space),
            out_shape=jax.ShapeDtypeStruct((blocks * BLOCK // 2, LANES), BF16),
            in_specs=[SMEM, SMEM, SMEM, VMEM, VMEM],
            out_specs=VMEM,
            compiler_params=params(16),
            name="attend",
        )(target.reshape(1), base, neighbours, query, extended)
        if k:
            route = [(i, (i ^ k) if pairs else (i + k) % mp) for i in range(mp)]
            chunk = lax.ppermute(chunk, "mp", route)
        received.append(chunk)
        heads.append(source)
    return pl.pallas_call(
        functools.partial(mix_kernel, mp, head),
        out_shape=jax.ShapeDtypeStruct((tok // mp, w_out.shape[1]), BF16),
        in_specs=[SMEM] + [VMEM] * (mp + 1),
        out_specs=VMEM,
        scratch_shapes=[pltpu.VMEM((mp, blocks * BLOCK // 2, LANES), BF16)],
        compiler_params=params(16),
        name="mix",
    )(jnp.stack(heads), *received, w_out)


def solution(mesh):
    placed = (
        P("space", None),
        P(),
        P(None, "mp", None),
        P(),
        P("mp"),
        P("space"),
        P("space", None),
    )
    return jax.shard_map(
        per_device, mesh=mesh, in_specs=placed, out_specs=P(("space", "mp"), None), check_vma=False
    )
```

```python
import functools

import jax
import jax.numpy as jnp
from jax import lax
from jax.experimental import pallas as pl
from jax.experimental.pallas import tpu as pltpu
from jax.sharding import PartitionSpec as P

BLOCK = 128
REACH = 6
LANES = 128
TILE = 256
F32 = jnp.float32
BF16 = jnp.bfloat16


def dot(a, b):
    return jnp.dot(a, b, preferred_element_type=F32)


def dot_nt(a, b):
    return lax.dot_general(a, b, (((1,), (1,)), ((), ())), preferred_element_type=F32)


def iota(shape, dim):
    return lax.broadcasted_iota(jnp.int32, shape, dim)


def send_kernel(space, compact, scale_ref, tokens_hbm, gain_hbm, w_hbm, slots_hbm, *refs):
    outs = refs[:-8]
    tok_buf, norm_buf, factor_buf = refs[-8:-5]
    w_buf, gain_buf, slots_buf, packed_buf, sems = refs[-5:]
    tok, width = tokens_hbm.shape
    tiles = tok // TILE
    group = tok // space
    head = w_hbm.shape[0] // 3
    slot_rows = slots_hbm.shape[0]
    rows = slots_buf.shape[0]
    small = [
        pltpu.make_async_copy(slots_hbm, slots_buf.at[pl.ds(0, slot_rows), :], sems.at[tiles]),
        pltpu.make_async_copy(gain_hbm, gain_buf, sems.at[tiles + 1]),
        pltpu.make_async_copy(w_hbm, w_buf, sems.at[tiles + 2]),
    ]
    copies = [
        pltpu.make_async_copy(
            tokens_hbm.at[pl.ds(i * TILE, TILE), :], tok_buf.at[pl.ds(i * TILE, TILE), :], sems.at[i]
        )
        for i in range(tiles)
    ]
    for copy in small[:2] + copies[:1] + small[2:] + copies[1:]:
        copy.start()

    small[0].wait()
    slots = jnp.where(iota((rows, LANES), 0) < slot_rows, slots_buf[...], -1)
    masks = [((slots >= d * tok) & (slots < (d + 1) * tok)) for d in range(space)]
    ones = [m.astype(F32) for m in masks]
    stacked = jnp.concatenate(ones, axis=0).astype(BF16)
    total_rows = rows * space
    earlier = (iota((LANES, LANES), 0) < iota((LANES, LANES), 1)).astype(F32).astype(BF16)
    in_row = dot(stacked, earlier)
    row_total = dot(stacked, jnp.ones((LANES, LANES), BF16)).astype(BF16)
    left, right = iota((total_rows, total_rows), 0), iota((total_rows, total_rows), 1)
    above = ((left // rows == right // rows) & (right < left)).astype(F32).astype(BF16)
    rank = in_row + dot(above, row_total)
    pos = jnp.full((rows, LANES), -1.0, F32)
    place = slots
    for d in range(space):
        pos = jnp.where(masks[d], rank[d * rows : (d + 1) * rows] + float(d * group), pos)
        place = jnp.where(masks[d], slots - d * tok, place)
    slots_buf[...] = pos.astype(jnp.int32)
    high = (place >> 7).astype(F32)
    low = (place & 127).astype(F32)
    for copy in small[1:]:
        copy.wait()
    gain = gain_buf[...]
    scale = scale_ref[0]
    piece = 16
    row16 = iota((16, LANES), 0)

    def measure(n, carry):
        at = pl.ds(pl.multiple_of(n * piece, piece), piece)
        values = tok_buf[at, :].astype(F32)
        mean_square = jnp.mean(values * values, axis=1, keepdims=True)
        factor_buf[at, :] = jnp.broadcast_to(lax.rsqrt(mean_square + 1e-05), (piece, LANES))
        return carry

    def normalize(i):
        for start in range(i * TILE, (i + 1) * TILE, piece):
            at = slice(start, start + piece)
            factor = factor_buf[at, :]
            for c in range(0, width, LANES):
                norm_buf[at, c : c + LANES] = (
                    tok_buf[at, c : c + LANES].astype(F32) * factor * gain[:, c : c + LANES]
                ).astype(BF16)

    def project(i):
        rows_of = norm_buf[i * TILE : (i + 1) * TILE, :]
        projected = dot_nt(w_buf[...], rows_of)
        at = slice(i * TILE, (i + 1) * TILE)
        query, key = projected[:head], projected[head : 2 * head]
        query = query * (
            scale * lax.rsqrt(jnp.sum(query * query, axis=0, keepdims=True) + 1e-06)
        )
        key = key * lax.rsqrt(jnp.sum(key * key, axis=0, keepdims=True) + 1e-06)
        packed_buf[:head, at] = key.astype(BF16)
        packed_buf[head : 2 * head, at] = projected[2 * head :].astype(BF16)
        packed_buf[2 * head : 3 * head, at] = query.astype(BF16)

    for r in range(tok // LANES):
        packed_buf[3 * head : 3 * head + 16, r * LANES : (r + 1) * LANES] = jnp.where(
            row16 == 0,
            high[r : r + 1],
            jnp.where(row16 == 1, low[r : r + 1], 0.0),
        ).astype(BF16)
    packed_buf[3 * head + 16 :, :] = jnp.zeros((TILE - 3 * head - 16, tok), BF16)
    per = TILE // piece
    for i in range(tiles):
        copies[i].wait()
        lax.fori_loop(i * per, (i + 1) * per, measure, 0, unroll=8)
        if i:
            project(i - 1)
        normalize(i)
    project(tiles - 1)

    def chosen_rows(starts, count):
        wanted = jnp.concatenate([iota((count, LANES), 0) + start for start in starts], axis=0)
        chosen = jnp.concatenate(
            [
                (wanted == slots_buf[r : r + 1, :]).astype(F32).astype(BF16)
                for r in range(tok // LANES)
            ],
            axis=1,
        )
        return dot_nt(chosen, packed_buf[...])

    if compact:
        me = lax.axis_index("space")
        half = group // 2
        part = iota((half, LANES), 1)
        row8, lane8 = iota((8, LANES), 0), iota((8, LANES), 1)
        pick = (lane8 == head + (row8 & 1)).astype(F32).astype(BF16)
        for k in range(0, space, 2):
            both_sent = chosen_rows([(me ^ k) * group, (me ^ (k + 1)) * group], group)
            for n in range(2):
                sent = both_sent[n * group : (n + 1) * group]
                out = outs[k + n]
                out[:group, :] = sent[:, :LANES].astype(BF16)
                query = sent[:, LANES:]
                out[group : group + half, :] = jnp.where(
                    part < head, query[:half], pltpu.roll(query[half:], head, 1)
                ).astype(BF16)
                query = query.astype(BF16)
                spots = dot_nt(pick, query[:LANES])
                more = jnp.concatenate(
                    [query[LANES:], jnp.zeros((2 * LANES - group, LANES), BF16)], axis=0
                )
                out[group + half :, :] = jnp.where(
                    row8 < 2, spots, dot_nt(pick, more)
                ).astype(BF16)
    else:
        step = 384

        def permute(n, carry):
            start = pl.multiple_of(n * step, step)
            outs[0][pl.ds(start, step), :] = chosen_rows([start], step).astype(BF16)
            return carry

        lax.fori_loop(0, tok // step, permute, 0)


def nest_kernel(head, compact, *refs):
    if compact:
        count = len(refs) - 4
        chunks, (first_ref, last_ref, q_ref, got_ref) = refs[:count], refs[count:]
        group = got_ref.shape[0] // count
        half = group // 2
        rest = group - LANES
        part = iota((half, LANES), 1)
        line = iota((1, LANES), 1)
        spots, tails = [], []
        for k in range(count):
            query = chunks[k][group : group + half, :].astype(F32)
            near = jnp.where(part < head, query, 0.0).astype(BF16)
            far = jnp.where(part < head, pltpu.roll(query, head, 1), 0.0).astype(BF16)
            at, tail = k * LANES, count * LANES + k * rest
            got_ref[at : at + LANES, :LANES] = chunks[k][:LANES, :]
            got_ref[tail : tail + rest, :LANES] = chunks[k][LANES:group, :]
            got_ref[at : at + half, LANES:] = near
            got_ref[at + half : at + LANES, LANES:] = far[: LANES - half]
            got_ref[tail : tail + rest, LANES:] = far[LANES - half :]
            where = chunks[k][group + half :, :].astype(F32)
            spots.append(where[0:1] * float(BLOCK) + where[1:2])
            tails.append(where[2:3] * float(BLOCK) + where[3:4])
        for k in range(0, count, 2):
            spots.append(jnp.where(line < rest, tails[k], pltpu.roll(tails[k + 1], rest, 1)))
        slots = jnp.concatenate(spots, axis=1).astype(jnp.int32)
    else:
        got_ref, first_ref, last_ref, q_ref = refs
        lane, row = iota((8, LANES), 1), iota((8, LANES), 0)
        pick = (lane == row + head).astype(F32).astype(BF16)
        parts = dot_nt(pick, got_ref[:, LANES:])
        slots = (parts[0:1] * float(BLOCK) + parts[1:2]).astype(jnp.int32)
    tok = got_ref.shape[0]
    step = 384
    keep = iota((step, LANES), 1) < head
    edge = first_ref.shape[0]
    for start in range(0, tok, step):
        chosen = (iota((step, tok), 0) + start == slots).astype(F32).astype(BF16)
        nested = dot(chosen, got_ref[...])
        target, at = (first_ref, start) if start < edge else (last_ref, start - edge)
        target[at : at + step, :] = nested[:, :LANES].astype(BF16)
        q_ref[start : start + step, :] = jnp.where(keep, nested[:, LANES:], 0.0).astype(BF16)


def bias_of(near_ref, region_blocks, bias_ref):
    near = near_ref[...]
    blocks, slots = near.shape
    all_blocks = region_blocks * lax.axis_size("space")
    at = near - lax.axis_index("space") * region_blocks
    at = jnp.where(at >= all_blocks // 2, at - all_blocks, at)
    at = jnp.where(at < -(all_blocks // 2), at + all_blocks, at)
    at = jnp.where(near >= 0, at + REACH, -1)
    lane = iota((blocks, LANES), 1)
    bias = jnp.full((blocks, LANES), -1e30, F32)
    for s in range(slots):
        bias = jnp.where(lane == at[:, s : s + 1], 0.0, bias)
    for j in range(region_blocks + 2 * REACH):
        bias_ref[:, j * BLOCK : (j + 1) * BLOCK] = jnp.broadcast_to(
            bias[:, j : j + 1], (blocks, BLOCK)
        )


def attend_tiles(query, keys, bias_ref, b, first):
    scores = dot_nt(query, keys)
    return [
        scores[:, n * BLOCK : (n + 1) * BLOCK]
        + bias_ref[b : b + 1, (first + n) * BLOCK : (first + n + 1) * BLOCK]
        for n in range(keys.shape[0] // BLOCK)
    ]


def largest(parts):
    return jnp.max(functools.reduce(jnp.maximum, parts), axis=1, keepdims=True)


def weigh(parts, top, keys):
    exps = [jnp.exp(part - top) for part in parts]
    total = jnp.sum(functools.reduce(jnp.add, exps), axis=1, keepdims=True)
    weights = jnp.concatenate([e.astype(BF16) for e in exps], axis=1)
    return dot(weights, keys), total


def local_kernel(near_ref, q_ref, first_ref, last_ref, acc_ref, top_ref, total_ref, bias_ref):
    region_blocks = q_ref.shape[0] // BLOCK
    edge = first_ref.shape[0] // BLOCK
    bias_of(near_ref, region_blocks, bias_ref)

    def keys_of(low, high):
        parts = []
        if low < edge:
            parts.append(first_ref[low * BLOCK : min(high, edge) * BLOCK, :])
        if high > edge:
            parts.append(last_ref[max(low - edge, 0) * BLOCK : (high - edge) * BLOCK, :])
        return parts[0] if len(parts) == 1 else jnp.concatenate(parts, axis=0)

    def score(b):
        low, high = max(0, b - REACH), min(region_blocks, b + REACH + 1)
        keys = keys_of(low, high)
        query = q_ref[b * BLOCK : (b + 1) * BLOCK, :]
        return attend_tiles(query, keys, bias_ref, b, low + REACH), keys

    ahead = score(0)
    for b in range(region_blocks):
        (parts, keys), ahead = ahead, (score(b + 1) if b + 1 < region_blocks else None)
        top = largest(parts)
        values, total = weigh(parts, top, keys)
        at = slice(b * BLOCK, (b + 1) * BLOCK)
        acc_ref[at, :] = values
        top_ref[at, :] = jnp.broadcast_to(top, (BLOCK, LANES))
        total_ref[at, :] = jnp.broadcast_to(total, (BLOCK, LANES))


def halo_kernel(head, mp, q_ref, before_ref, after_ref, acc_ref, top_ref, total_ref, bias_ref,
                out_ref):
    region_blocks = q_ref.shape[0] // BLOCK
    blocks = region_blocks // mp
    half = blocks * BLOCK // 2
    lane = iota((half, LANES), 1)
    outputs = []
    for b in range(region_blocks):
        at = slice(b * BLOCK, (b + 1) * BLOCK)
        query = q_ref[at, :]
        sides = []
        if b < REACH:
            sides.append((before_ref[b * BLOCK :, :], b))
        if b + REACH >= region_blocks:
            count = b + REACH + 1 - region_blocks
            sides.append((after_ref[: count * BLOCK, :], region_blocks + REACH))
        scored = [attend_tiles(query, keys, bias_ref, b, first) for keys, first in sides]
        old = top_ref[at, :]
        top = old
        for parts in scored:
            top = jnp.maximum(top, largest(parts))
        keep = jnp.exp(old - top)
        values, total = acc_ref[at, :] * keep, total_ref[at, :] * keep
        for (keys, _), parts in zip(sides, scored):
            more, added = weigh(parts, top, keys)
            values, total = values + more, total + added
        outputs.append(values / total)
        if (b + 1) % blocks == 0:
            rows = jnp.concatenate(outputs, axis=0)
            outputs = []
            out_ref[shift_to(b // blocks)] = jnp.where(
                lane < head, pltpu.roll(rows[:half], head, 1), rows[half:]
            ).astype(BF16)


def shift_to(target):
    mp = lax.axis_size("mp")
    me = lax.axis_index("mp")
    return (me ^ target) if mp & (mp - 1) == 0 else lax.rem(target + mp - me, mp)


def source_of(shift):
    mp = lax.axis_size("mp")
    me = lax.axis_index("mp")
    return (me ^ shift) if mp & (mp - 1) == 0 else lax.rem(me + (mp - shift), mp)


def mix_kernel(shifts, head, *refs):
    mp = len(shifts)
    parts, w_ref, out_hbm, buf, out_buf, sems = refs[:mp], *refs[mp:]
    half = parts[0].shape[0]
    for shift, part in zip(shifts, parts):
        buf[source_of(shift)] = part[...]
    lane = iota((half, LANES), 1)
    upper, lower = [], []
    for pair in range(mp // 2):
        a = buf[2 * pair].astype(F32)
        b = buf[2 * pair + 1].astype(F32)
        upper.append(jnp.where(lane < head, a, pltpu.roll(b, head, 1)).astype(BF16))
        lower.append(jnp.where(lane < head, pltpu.roll(a, head, 1), b).astype(BF16))
    weights = w_ref[...]
    copies = []
    for n, rows in enumerate((upper, lower)):
        span = pl.ds(n * half, half)
        out_buf[span, :] = dot(jnp.concatenate(rows, axis=1), weights).astype(BF16)
        copies.append(
            pltpu.make_async_copy(out_buf.at[span, :], out_hbm.at[span, :], sems.at[n])
        )
        copies[-1].start()
    for copy in copies:
        copy.wait()


VMEM = pl.BlockSpec(memory_space=pltpu.VMEM)
SMEM = pl.BlockSpec(memory_space=pltpu.SMEM)
HBM = pl.BlockSpec(memory_space=pltpu.HBM)


def params(mib):
    return pltpu.CompilerParams(vmem_limit_bytes=mib << 20)


def per_device(tokens, norm_gain, w_qkv, w_out, head_scale, cycle_to_nested, neighbours):
    tok, width = tokens.shape
    space, mp = lax.axis_size("space"), lax.axis_size("mp")
    head = w_qkv.shape[2] // 3
    group = tok // space
    row_count = -(-tok // (8 * LANES)) * 8
    compact = space in (2, 4, 8) and group == LANES + LANES // 2
    chunk_rows = group + group // 2 + 8
    sent = pl.pallas_call(
        functools.partial(send_kernel, space, compact),
        out_shape=(jax.ShapeDtypeStruct((chunk_rows, LANES), BF16),) * space
        if compact
        else (jax.ShapeDtypeStruct((tok, TILE), BF16),),
        in_specs=[SMEM] + [HBM] * 4,
        out_specs=(VMEM,) * (space if compact else 1),
        scratch_shapes=[
            pltpu.VMEM((tok, width), BF16),
            pltpu.VMEM((tok, width), BF16),
            pltpu.VMEM((tok, LANES), F32),
            pltpu.VMEM((3 * head, width), BF16),
            pltpu.VMEM((1, width), F32),
            pltpu.VMEM((row_count, LANES), jnp.int32),
            pltpu.VMEM((TILE, tok), BF16),
            pltpu.SemaphoreType.DMA((tok // TILE + 3,)),
        ],
        compiler_params=params(24),
        name="send",
    )(
        head_scale,
        *(
            pltpu.with_memory_space_constraint(x, pltpu.HBM)
            for x in (
                tokens,
                norm_gain.reshape(1, width),
                w_qkv.reshape(width, 3 * head).T,
                cycle_to_nested.reshape(tok // LANES, LANES),
            )
        ),
    )
    edge = REACH * BLOCK
    if compact:
        got = [sent[0]]
        for k in range(1, space):
            got.append(lax.ppermute(sent[k], "space", [(i, i ^ k) for i in range(space)]))
    else:
        got = [
            lax.all_to_all(
                sent[0].reshape(space, group, TILE), "space", 0, 0, tiled=True
            ).reshape(tok, TILE)
        ]
    first, last, query = pl.pallas_call(
        functools.partial(nest_kernel, head, compact),
        out_shape=(
            jax.ShapeDtypeStruct((edge, LANES), BF16),
            jax.ShapeDtypeStruct((tok - edge, LANES), BF16),
            jax.ShapeDtypeStruct((tok, LANES), BF16),
        ),
        in_specs=[VMEM] * len(got),
        out_specs=(VMEM,) * 3,
        scratch_shapes=[pltpu.VMEM((tok, TILE), BF16)] if compact else [],
        compiler_params=params(16),
        name="nest",
    )(*got)
    up = [(i, (i + 1) % space) for i in range(space)]
    down = [(j, i) for i, j in up]
    before = lax.ppermute(last[last.shape[0] - edge :], "space", up)
    after = lax.ppermute(first, "space", down)
    region_blocks = tok // BLOCK
    blocks = region_blocks // mp
    state = pl.pallas_call(
        local_kernel,
        out_shape=[jax.ShapeDtypeStruct((tok, LANES), F32)] * 3
        + [jax.ShapeDtypeStruct((region_blocks, (region_blocks + 2 * REACH) * BLOCK), F32)],
        in_specs=[VMEM] * 4,
        out_specs=[VMEM] * 4,
        compiler_params=params(24),
        name="local",
    )(neighbours, query, first, last)
    order = list(range(mp))
    parts = pl.pallas_call(
        functools.partial(halo_kernel, head, mp),
        out_shape=jax.ShapeDtypeStruct((mp, blocks * BLOCK // 2, LANES), BF16),
        in_specs=[VMEM] * 7,
        out_specs=VMEM,
        compiler_params=params(24),
        name="halo",
    )(query, before, after, *state)
    received = [parts[0]]
    xor = mp & (mp - 1) == 0
    for k in order[1:]:
        route = [(i, (i ^ k) if xor else (i + k) % mp) for i in range(mp)]
        received.append(lax.ppermute(parts[k], "mp", route))
    out_shape = (tok // mp, w_out.shape[1])
    return pl.pallas_call(
        functools.partial(mix_kernel, order, head),
        out_shape=jax.ShapeDtypeStruct(out_shape, BF16),
        in_specs=[VMEM] * (mp + 1),
        out_specs=HBM,
        scratch_shapes=[
            pltpu.VMEM((mp, blocks * BLOCK // 2, LANES), BF16),
            pltpu.VMEM(out_shape, BF16),
            pltpu.SemaphoreType.DMA((2,)),
        ],
        compiler_params=params(16),
        name="mix",
    )(*received, w_out)


def solution(mesh):
    placed = (
        P("space", None),
        P(),
        P(None, "mp", None),
        P(),
        P("mp"),
        P("space"),
        P("space", None),
    )
    return jax.shard_map(
        per_device, mesh=mesh, in_specs=placed, out_specs=P(("space", "mp"), None), check_vma=False
    )
```

```python
import functools

import jax
import jax.numpy as jnp
from jax import lax
from jax.experimental import pallas as pl
from jax.experimental.pallas import tpu as pltpu
from jax.sharding import PartitionSpec as P

BLOCK = 128
REACH = 6
LANES = 128
TILE = 256
AHEAD = 2
F32 = jnp.float32
BF16 = jnp.bfloat16


def dot(a, b):
    return jnp.dot(a, b, preferred_element_type=F32)


def dot_nt(a, b):
    return lax.dot_general(a, b, (((1,), (1,)), ((), ())), preferred_element_type=F32)


def iota(shape, dim):
    return lax.broadcasted_iota(jnp.int32, shape, dim)


def send_kernel(space, compact, scale_ref, tokens_hbm, gain_hbm, w_hbm, slots_hbm, *refs):
    tok, width = tokens_hbm.shape
    tiles = tok // TILE
    outs, bufs = refs[: -5 - 3 * tiles], refs[-5 - 3 * tiles : -5]
    tok_bufs, norm_bufs, factor_bufs = (bufs[n * tiles : (n + 1) * tiles] for n in range(3))
    w_buf, gain_buf, slots_buf, packed_buf, sems = refs[-5:]
    group = tok // space
    head = w_hbm.shape[0] // 3
    slot_rows = slots_hbm.shape[0]
    rows = slots_buf.shape[0]
    small = [
        pltpu.make_async_copy(slots_hbm, slots_buf.at[pl.ds(0, slot_rows), :], sems.at[tiles]),
        pltpu.make_async_copy(gain_hbm, gain_buf, sems.at[tiles + 1]),
        pltpu.make_async_copy(w_hbm, w_buf, sems.at[tiles + 2]),
    ]
    copies = [
        pltpu.make_async_copy(
            tokens_hbm.at[pl.ds(i * TILE, TILE), :], tok_bufs[i], sems.at[i]
        )
        for i in range(tiles)
    ]
    for copy in small[:2] + copies[:1] + small[2:] + copies[1:]:
        copy.start()

    small[0].wait()
    slots = jnp.where(iota((rows, LANES), 0) < slot_rows, slots_buf[...], -1)
    masks = [((slots >= d * tok) & (slots < (d + 1) * tok)) for d in range(space)]
    ones = [m.astype(F32) for m in masks]
    stacked = jnp.concatenate(ones, axis=0).astype(BF16)
    total_rows = rows * space
    earlier = (iota((LANES, LANES), 0) < iota((LANES, LANES), 1)).astype(F32).astype(BF16)
    in_row = dot(stacked, earlier)
    row_total = dot(stacked, jnp.ones((LANES, LANES), BF16)).astype(BF16)
    left, right = iota((total_rows, total_rows), 0), iota((total_rows, total_rows), 1)
    above = ((left // rows == right // rows) & (right < left)).astype(F32).astype(BF16)
    rank = in_row + dot(above, row_total)
    pos = jnp.full((rows, LANES), -1.0, F32)
    place = slots
    for d in range(space):
        pos = jnp.where(masks[d], rank[d * rows : (d + 1) * rows] + float(d * group), pos)
        place = jnp.where(masks[d], slots - d * tok, place)
    slots_buf[...] = pos.astype(jnp.int32)
    high = (place >> 7).astype(F32)
    low = (place & 127).astype(F32)
    for copy in small[1:]:
        copy.wait()
    gain = gain_buf[...]
    scale = scale_ref[0]
    piece = 16
    row16 = iota((16, LANES), 0)

    zero = jnp.minimum(lax.axis_index("space"), 0)

    def measure(i):
        for start in range(0, TILE, piece):
            at = slice(start, start + piece)
            values = tok_bufs[i][at, :].astype(F32)
            mean_square = jnp.mean(values * values, axis=1, keepdims=True)
            factor_bufs[i][at, :] = jnp.broadcast_to(
                lax.rsqrt(mean_square + 1e-05), (piece, LANES)
            )

    def normalize(i):
        for start in range(0, TILE, piece):
            at = slice(start, start + piece)
            again = pl.ds(pl.multiple_of(zero + start, piece), piece)
            factor = factor_bufs[i][at, :]
            for c in range(0, width, LANES):
                norm_bufs[i][at, c : c + LANES] = (
                    tok_bufs[i][again, c : c + LANES].astype(F32)
                    * factor
                    * gain[:, c : c + LANES]
                ).astype(BF16)

    def project(i):
        projected = dot_nt(w_buf[...], norm_bufs[i][...])
        at = slice(i * TILE, (i + 1) * TILE)
        query, key = projected[:head], projected[head : 2 * head]
        query = query * (
            scale * lax.rsqrt(jnp.sum(query * query, axis=0, keepdims=True) + 1e-06)
        )
        key = key * lax.rsqrt(jnp.sum(key * key, axis=0, keepdims=True) + 1e-06)
        packed_buf[:head, at] = key.astype(BF16)
        packed_buf[head : 2 * head, at] = projected[2 * head :].astype(BF16)
        packed_buf[2 * head : 3 * head, at] = query.astype(BF16)

    for r in range(tok // LANES):
        packed_buf[3 * head : 3 * head + 16, r * LANES : (r + 1) * LANES] = jnp.where(
            row16 == 0,
            high[r : r + 1],
            jnp.where(row16 == 1, low[r : r + 1], 0.0),
        ).astype(BF16)
    packed_buf[3 * head + 16 :, :] = jnp.zeros((TILE - 3 * head - 16, tok), BF16)
    for i in range(tiles):
        copies[i].wait()
        if i:
            project(i - 1)
        measure(i)
        normalize(i)
    project(tiles - 1)

    def chosen_rows(starts, count):
        wanted = jnp.concatenate([iota((count, LANES), 0) + start for start in starts], axis=0)
        chosen = jnp.concatenate(
            [
                (wanted == slots_buf[r : r + 1, :]).astype(F32).astype(BF16)
                for r in range(tok // LANES)
            ],
            axis=1,
        )
        return dot_nt(chosen, packed_buf[...])

    if compact:
        me = lax.axis_index("space")
        half = group // 2
        part = iota((half, LANES), 1)
        row8, lane8 = iota((8, LANES), 0), iota((8, LANES), 1)
        pick = (lane8 == head + (row8 & 1)).astype(F32).astype(BF16)
        for k in range(0, space, 2):
            both_sent = chosen_rows([(me ^ k) * group, (me ^ (k + 1)) * group], group)
            for n in range(2):
                sent = both_sent[n * group : (n + 1) * group]
                out = outs[k + n]
                out[:group, :] = sent[:, :LANES].astype(BF16)
                query = sent[:, LANES:]
                out[group : group + half, :] = jnp.where(
                    part < head, query[:half], pltpu.roll(query[half:], head, 1)
                ).astype(BF16)
                query = query.astype(BF16)
                spots = dot_nt(pick, query[:LANES])
                more = jnp.concatenate(
                    [query[LANES:], jnp.zeros((2 * LANES - group, LANES), BF16)], axis=0
                )
                out[group + half :, :] = jnp.where(
                    row8 < 2, spots, dot_nt(pick, more)
                ).astype(BF16)
    else:
        step = 384

        def permute(n, carry):
            start = pl.multiple_of(n * step, step)
            outs[0][pl.ds(start, step), :] = chosen_rows([start], step).astype(BF16)
            return carry

        lax.fori_loop(0, tok // step, permute, 0)


def nest_kernel(head, compact, *refs):
    if compact:
        count = len(refs) - 4
        chunks, (first_ref, last_ref, q_ref, got_ref) = refs[:count], refs[count:]
        group = got_ref.shape[0] // count
        half = group // 2
        rest = group - LANES
        part = iota((half, LANES), 1)
        line = iota((1, LANES), 1)
        spots, tails = [], []
        for k in range(count):
            query = chunks[k][group : group + half, :].astype(F32)
            near = jnp.where(part < head, query, 0.0).astype(BF16)
            far = jnp.where(part < head, pltpu.roll(query, head, 1), 0.0).astype(BF16)
            at, tail = k * LANES, count * LANES + k * rest
            got_ref[at : at + LANES, :LANES] = chunks[k][:LANES, :]
            got_ref[tail : tail + rest, :LANES] = chunks[k][LANES:group, :]
            got_ref[at : at + half, LANES:] = near
            got_ref[at + half : at + LANES, LANES:] = far[: LANES - half]
            got_ref[tail : tail + rest, LANES:] = far[LANES - half :]
            where = chunks[k][group + half :, :].astype(F32)
            spots.append(where[0:1] * float(BLOCK) + where[1:2])
            tails.append(where[2:3] * float(BLOCK) + where[3:4])
        for k in range(0, count, 2):
            spots.append(jnp.where(line < rest, tails[k], pltpu.roll(tails[k + 1], rest, 1)))
        slots = jnp.concatenate(spots, axis=1).astype(jnp.int32)
    else:
        got_ref, first_ref, last_ref, q_ref = refs
        lane, row = iota((8, LANES), 1), iota((8, LANES), 0)
        pick = (lane == row + head).astype(F32).astype(BF16)
        parts = dot_nt(pick, got_ref[:, LANES:])
        slots = (parts[0:1] * float(BLOCK) + parts[1:2]).astype(jnp.int32)
    tok = got_ref.shape[0]
    step = 384
    keep = iota((step, LANES), 1) < head
    edge = first_ref.shape[0]
    for start in range(0, tok, step):
        chosen = (iota((step, tok), 0) + start == slots).astype(F32).astype(BF16)
        nested = dot(chosen, got_ref[...])
        target, at = (first_ref, start) if start < edge else (last_ref, start - edge)
        target[at : at + step, :] = nested[:, :LANES].astype(BF16)
        q_ref[start : start + step, :] = jnp.where(keep, nested[:, LANES:], 0.0).astype(BF16)


def bias_of(near_ref, region_blocks, bias_ref):
    near = near_ref[...]
    blocks, slots = near.shape
    all_blocks = region_blocks * lax.axis_size("space")
    at = near - lax.axis_index("space") * region_blocks
    at = jnp.where(at >= all_blocks // 2, at - all_blocks, at)
    at = jnp.where(at < -(all_blocks // 2), at + all_blocks, at)
    at = jnp.where(near >= 0, at + REACH, -1)
    lane = iota((blocks, LANES), 1)
    bias = jnp.full((blocks, LANES), -1e30, F32)
    for s in range(slots):
        bias = jnp.where(lane == at[:, s : s + 1], 0.0, bias)
    for j in range(region_blocks + 2 * REACH):
        bias_ref[:, j * BLOCK : (j + 1) * BLOCK] = jnp.broadcast_to(
            bias[:, j : j + 1], (blocks, BLOCK)
        )


def attend_tiles(query, keys, bias_ref, b, first):
    scores = dot_nt(query, keys)
    return [
        scores[:, n * BLOCK : (n + 1) * BLOCK]
        + bias_ref[b : b + 1, (first + n) * BLOCK : (first + n + 1) * BLOCK]
        for n in range(keys.shape[0] // BLOCK)
    ]


def largest(parts):
    return jnp.max(functools.reduce(jnp.maximum, parts), axis=1, keepdims=True)


def weigh(parts, top, keys):
    exps = [jnp.exp(part - top) for part in parts]
    total = jnp.sum(functools.reduce(jnp.add, exps), axis=1, keepdims=True)
    weights = jnp.concatenate([e.astype(BF16) for e in exps], axis=1)
    return dot(weights, keys), total


def local_kernel(near_ref, q_ref, first_ref, last_ref, acc_ref, top_ref, total_ref, bias_ref):
    region_blocks = q_ref.shape[0] // BLOCK
    edge = first_ref.shape[0] // BLOCK
    bias_of(near_ref, region_blocks, bias_ref)

    def keys_of(low, high):
        parts = []
        if low < edge:
            parts.append(first_ref[low * BLOCK : min(high, edge) * BLOCK, :])
        if high > edge:
            parts.append(last_ref[max(low - edge, 0) * BLOCK : (high - edge) * BLOCK, :])
        return parts[0] if len(parts) == 1 else jnp.concatenate(parts, axis=0)

    def score(b):
        low, high = max(0, b - REACH), min(region_blocks, b + REACH + 1)
        keys = keys_of(low, high)
        query = q_ref[b * BLOCK : (b + 1) * BLOCK, :]
        return attend_tiles(query, keys, bias_ref, b, low + REACH), keys

    ahead = score(0)
    for b in range(region_blocks):
        (parts, keys), ahead = ahead, (score(b + 1) if b + 1 < region_blocks else None)
        top = largest(parts)
        values, total = weigh(parts, top, keys)
        at = slice(b * BLOCK, (b + 1) * BLOCK)
        acc_ref[at, :] = values
        top_ref[at, :] = jnp.broadcast_to(top, (BLOCK, LANES))
        total_ref[at, :] = jnp.broadcast_to(total, (BLOCK, LANES))


def halo_kernel(head, mp, q_ref, before_ref, after_ref, acc_ref, top_ref, total_ref, bias_ref,
                out_ref):
    region_blocks = q_ref.shape[0] // BLOCK
    blocks = region_blocks // mp
    half = blocks * BLOCK // 2
    lane = iota((half, LANES), 1)

    def score(b):
        query = q_ref[b * BLOCK : (b + 1) * BLOCK, :]
        sides = []
        if b < REACH:
            sides.append((before_ref[b * BLOCK :, :], b))
        if b + REACH >= region_blocks:
            count = b + REACH + 1 - region_blocks
            sides.append((after_ref[: count * BLOCK, :], region_blocks + REACH))
        return sides, [attend_tiles(query, keys, bias_ref, b, first) for keys, first in sides]

    outputs = []
    queue = [score(b) for b in range(AHEAD)]
    for b in range(region_blocks):
        if b + AHEAD < region_blocks:
            queue.append(score(b + AHEAD))
        sides, scored = queue.pop(0)
        at = slice(b * BLOCK, (b + 1) * BLOCK)
        old = top_ref[at, :]
        top = old
        for parts in scored:
            top = jnp.maximum(top, largest(parts))
        keep = jnp.exp(old - top)
        values, total = acc_ref[at, :] * keep, total_ref[at, :] * keep
        for (keys, _), parts in zip(sides, scored):
            more, added = weigh(parts, top, keys)
            values, total = values + more, total + added
        outputs.append(values / total)
        if (b + 1) % blocks == 0:
            rows = jnp.concatenate(outputs, axis=0)
            outputs = []
            out_ref[shift_to(b // blocks)] = jnp.where(
                lane < head, pltpu.roll(rows[:half], head, 1), rows[half:]
            ).astype(BF16)


def shift_to(target):
    mp = lax.axis_size("mp")
    me = lax.axis_index("mp")
    return (me ^ target) if mp & (mp - 1) == 0 else lax.rem(target + mp - me, mp)


def source_of(shift):
    mp = lax.axis_size("mp")
    me = lax.axis_index("mp")
    return (me ^ shift) if mp & (mp - 1) == 0 else lax.rem(me + (mp - shift), mp)


def mix_kernel(shifts, head, *refs):
    mp = len(shifts)
    parts, w_ref, out_hbm, buf, out_buf, sems = refs[:mp], *refs[mp:]
    half = parts[0].shape[0]
    for shift, part in zip(shifts, parts):
        buf[source_of(shift)] = part[...]
    lane = iota((half, LANES), 1)
    upper, lower = [], []
    for pair in range(mp // 2):
        a = buf[2 * pair].astype(F32)
        b = buf[2 * pair + 1].astype(F32)
        upper.append(jnp.where(lane < head, a, pltpu.roll(b, head, 1)).astype(BF16))
        lower.append(jnp.where(lane < head, pltpu.roll(a, head, 1), b).astype(BF16))
    weights = w_ref[...]
    copies = []
    for n, rows in enumerate((upper, lower)):
        span = pl.ds(n * half, half)
        out_buf[span, :] = dot(jnp.concatenate(rows, axis=1), weights).astype(BF16)
        copies.append(
            pltpu.make_async_copy(out_buf.at[span, :], out_hbm.at[span, :], sems.at[n])
        )
        copies[-1].start()
    for copy in copies:
        copy.wait()


VMEM = pl.BlockSpec(memory_space=pltpu.VMEM)
SMEM = pl.BlockSpec(memory_space=pltpu.SMEM)
HBM = pl.BlockSpec(memory_space=pltpu.HBM)


def params(mib):
    return pltpu.CompilerParams(vmem_limit_bytes=mib << 20)


def per_device(tokens, norm_gain, w_qkv, w_out, head_scale, cycle_to_nested, neighbours):
    tok, width = tokens.shape
    space, mp = lax.axis_size("space"), lax.axis_size("mp")
    head = w_qkv.shape[2] // 3
    group = tok // space
    row_count = -(-tok // (8 * LANES)) * 8
    compact = space in (2, 4, 8) and group == LANES + LANES // 2
    chunk_rows = group + group // 2 + 8
    sent = pl.pallas_call(
        functools.partial(send_kernel, space, compact),
        out_shape=(jax.ShapeDtypeStruct((chunk_rows, LANES), BF16),) * space
        if compact
        else (jax.ShapeDtypeStruct((tok, TILE), BF16),),
        in_specs=[SMEM] + [HBM] * 4,
        out_specs=(VMEM,) * (space if compact else 1),
        scratch_shapes=[
            *([pltpu.VMEM((TILE, width), BF16)] * (2 * tok // TILE)),
            *([pltpu.VMEM((TILE, LANES), F32)] * (tok // TILE)),
            pltpu.VMEM((3 * head, width), BF16),
            pltpu.VMEM((1, width), F32),
            pltpu.VMEM((row_count, LANES), jnp.int32),
            pltpu.VMEM((TILE, tok), BF16),
            pltpu.SemaphoreType.DMA((tok // TILE + 3,)),
        ],
        compiler_params=params(24),
        name="send",
    )(
        head_scale,
        *(
            pltpu.with_memory_space_constraint(x, pltpu.HBM)
            for x in (
                tokens,
                norm_gain.reshape(1, width),
                w_qkv.reshape(width, 3 * head).T,
                cycle_to_nested.reshape(tok // LANES, LANES),
            )
        ),
    )
    edge = REACH * BLOCK
    if compact:
        got = [sent[0]]
        for k in [7, 6, 5, 4, 3, 2, 1]:
            got.append(lax.ppermute(sent[k], "space", [(i, i ^ k) for i in range(space)]))
    else:
        got = [
            lax.all_to_all(
                sent[0].reshape(space, group, TILE), "space", 0, 0, tiled=True
            ).reshape(tok, TILE)
        ]
    first, last, query = pl.pallas_call(
        functools.partial(nest_kernel, head, compact),
        out_shape=(
            jax.ShapeDtypeStruct((edge, LANES), BF16),
            jax.ShapeDtypeStruct((tok - edge, LANES), BF16),
            jax.ShapeDtypeStruct((tok, LANES), BF16),
        ),
        in_specs=[VMEM] * len(got),
        out_specs=(VMEM,) * 3,
        scratch_shapes=[pltpu.VMEM((tok, TILE), BF16)] if compact else [],
        compiler_params=params(16),
        name="nest",
    )(*got)
    up = [(i, (i + 1) % space) for i in range(space)]
    down = [(j, i) for i, j in up]
    before = lax.ppermute(last[last.shape[0] - edge :], "space", up)
    after = lax.ppermute(first, "space", down)
    region_blocks = tok // BLOCK
    blocks = region_blocks // mp
    state = pl.pallas_call(
        local_kernel,
        out_shape=[jax.ShapeDtypeStruct((tok, LANES), F32)] * 3
        + [jax.ShapeDtypeStruct((region_blocks, (region_blocks + 2 * REACH) * BLOCK), F32)],
        in_specs=[VMEM] * 4,
        out_specs=[VMEM] * 4,
        compiler_params=params(24),
        name="local",
    )(neighbours, query, first, last)
    order = list(range(mp))
    parts = pl.pallas_call(
        functools.partial(halo_kernel, head, mp),
        out_shape=jax.ShapeDtypeStruct((mp, blocks * BLOCK // 2, LANES), BF16),
        in_specs=[VMEM] * 7,
        out_specs=VMEM,
        compiler_params=params(24),
        name="halo",
    )(query, before, after, *state)
    received = [parts[0]]
    xor = mp & (mp - 1) == 0
    for k in order[1:]:
        route = [(i, (i ^ k) if xor else (i + k) % mp) for i in range(mp)]
        received.append(lax.ppermute(parts[k], "mp", route))
    out_shape = (tok // mp, w_out.shape[1])
    return pl.pallas_call(
        functools.partial(mix_kernel, order, head),
        out_shape=jax.ShapeDtypeStruct(out_shape, BF16),
        in_specs=[VMEM] * (mp + 1),
        out_specs=HBM,
        scratch_shapes=[
            pltpu.VMEM((mp, blocks * BLOCK // 2, LANES), BF16),
            pltpu.VMEM(out_shape, BF16),
            pltpu.SemaphoreType.DMA((2,)),
        ],
        compiler_params=params(16),
        name="mix",
    )(*received, w_out)


def solution(mesh):
    placed = (
        P("space", None),
        P(),
        P(None, "mp", None),
        P(),
        P("mp"),
        P("space"),
        P("space", None),
    )
    return jax.shard_map(
        per_device, mesh=mesh, in_specs=placed, out_specs=P(("space", "mp"), None), check_vma=False
    )
```

```python
import functools

import jax
import jax.numpy as jnp
from jax import lax
from jax.experimental import pallas as pl
from jax.experimental.pallas import tpu as pltpu
from jax.sharding import PartitionSpec as P

BLOCK = 128
REACH = 6
LANES = 128
TILE = 256
AHEAD = 2
F32 = jnp.float32
BF16 = jnp.bfloat16


def dot(a, b):
    return jnp.dot(a, b, preferred_element_type=F32)


def dot_nt(a, b):
    return lax.dot_general(a, b, (((1,), (1,)), ((), ())), preferred_element_type=F32)


def iota(shape, dim):
    return lax.broadcasted_iota(jnp.int32, shape, dim)


def send_kernel(space, compact, scale_ref, tokens_hbm, gain_hbm, w_hbm, slots_hbm, *refs):
    tok, width = tokens_hbm.shape
    tiles = tok // TILE
    outs, bufs = refs[: -5 - 3 * tiles], refs[-5 - 3 * tiles : -5]
    tok_bufs, norm_bufs, factor_bufs = (bufs[n * tiles : (n + 1) * tiles] for n in range(3))
    w_buf, gain_buf, slots_buf, packed_buf, sems = refs[-5:]
    group = tok // space
    head = w_hbm.shape[0] // 3
    slot_rows = slots_hbm.shape[0]
    rows = slots_buf.shape[0]
    small = [
        pltpu.make_async_copy(slots_hbm, slots_buf.at[pl.ds(0, slot_rows), :], sems.at[tiles + 1]),
        pltpu.make_async_copy(gain_hbm, gain_buf, sems.at[tiles + 2]),
    ]
    spans = [(c, slice(c * LANES, (c + 1) * LANES)) for c in range(width // LANES)]

    def fetch(i):
        return [
            pltpu.make_async_copy(
                tokens_hbm.at[pl.ds(i * TILE, TILE), pl.ds(c * LANES, LANES)],
                tok_bufs[i].at[c],
                sems.at[i],
            )
            for c, _ in spans
        ]

    copies = [fetch(i) for i in range(tiles)]
    weight_copies = [
        pltpu.make_async_copy(
            w_hbm.at[:, pl.ds(c * LANES, LANES)],
            w_buf.at[c],
            sems.at[tiles],
        )
        for c, _ in spans
    ]
    for copy in small + copies[0] + weight_copies + sum(copies[1:], []):
        copy.start()

    small[0].wait()
    slots = jnp.where(iota((rows, LANES), 0) < slot_rows, slots_buf[...], -1)
    masks = [((slots >= d * tok) & (slots < (d + 1) * tok)) for d in range(space)]
    ones = [m.astype(F32) for m in masks]
    stacked = jnp.concatenate(ones, axis=0).astype(BF16)
    total_rows = rows * space
    earlier = (iota((LANES, LANES), 0) < iota((LANES, LANES), 1)).astype(F32).astype(BF16)
    in_row = dot(stacked, earlier)
    row_total = dot(stacked, jnp.ones((LANES, LANES), BF16)).astype(BF16)
    left, right = iota((total_rows, total_rows), 0), iota((total_rows, total_rows), 1)
    above = ((left // rows == right // rows) & (right < left)).astype(F32).astype(BF16)
    rank = in_row + dot(above, row_total)
    pos = jnp.full((rows, LANES), -1.0, F32)
    place = slots
    for d in range(space):
        pos = jnp.where(masks[d], rank[d * rows : (d + 1) * rows] + float(d * group), pos)
        place = jnp.where(masks[d], slots - d * tok, place)
    slots_buf[...] = pos.astype(jnp.int32)
    high = (place >> 7).astype(F32)
    low = (place & 127).astype(F32)
    small[1].wait()
    gain = gain_buf[...]
    scale = scale_ref[0]
    piece = 16
    row16 = iota((16, LANES), 0)

    zero = jnp.minimum(lax.axis_index("space"), 0)

    def measure(i):
        for start in range(0, TILE, piece):
            at = slice(start, start + piece)
            squares = []
            for c, _ in spans:
                values = tok_bufs[i][c, at, :].astype(F32)
                squares.append(values * values)
            while len(squares) > 1:
                squares = [x + y for x, y in zip(squares[::2], squares[1::2])]
            mean_square = jnp.sum(squares[0], axis=1, keepdims=True) / width
            factor_bufs[i][at, :] = jnp.broadcast_to(
                lax.rsqrt(mean_square + 1e-05), (piece, LANES)
            )

    def normalize(i):
        for start in range(0, TILE, piece):
            at = slice(start, start + piece)
            again = pl.ds(pl.multiple_of(zero + start, piece), piece)
            factor = factor_bufs[i][at, :]
            for c, span in spans:
                norm_bufs[i][c, at, :] = (
                    tok_bufs[i][c, again, :].astype(F32) * factor * gain[:, span]
                ).astype(BF16)

    def project(i):
        projected = dot_nt(
            jnp.concatenate([w_buf[c] for c, _ in spans], axis=1),
            jnp.concatenate([norm_bufs[i][c] for c, _ in spans], axis=1),
        )
        at = slice(i * TILE, (i + 1) * TILE)
        query, key = projected[:head], projected[head : 2 * head]
        query = query * (
            scale * lax.rsqrt(jnp.sum(query * query, axis=0, keepdims=True) + 1e-06)
        )
        key = key * lax.rsqrt(jnp.sum(key * key, axis=0, keepdims=True) + 1e-06)
        packed_buf[:head, at] = key.astype(BF16)
        packed_buf[head : 2 * head, at] = projected[2 * head :].astype(BF16)
        packed_buf[2 * head : 3 * head, at] = query.astype(BF16)

    for r in range(tok // LANES):
        packed_buf[3 * head : 3 * head + 16, r * LANES : (r + 1) * LANES] = jnp.where(
            row16 == 0,
            high[r : r + 1],
            jnp.where(row16 == 1, low[r : r + 1], 0.0),
        ).astype(BF16)
    packed_buf[3 * head + 16 :, :] = jnp.zeros((TILE - 3 * head - 16, tok), BF16)
    for i in range(tiles):
        pltpu.make_async_copy(tok_bufs[i], tok_bufs[i], sems.at[i]).wait()
        if i == 1:
            pltpu.make_async_copy(w_buf, w_buf, sems.at[tiles]).wait()
        if i:
            project(i - 1)
        measure(i)
        normalize(i)
    project(tiles - 1)

    def chosen_rows(starts, count):
        wanted = jnp.concatenate([iota((count, LANES), 0) + start for start in starts], axis=0)
        chosen = jnp.concatenate(
            [
                (wanted == slots_buf[r : r + 1, :]).astype(F32).astype(BF16)
                for r in range(tok // LANES)
            ],
            axis=1,
        )
        return dot_nt(chosen, packed_buf[...])

    if compact:
        me = lax.axis_index("space")
        half = group // 2
        part = iota((half, LANES), 1)
        row8, lane8 = iota((8, LANES), 0), iota((8, LANES), 1)
        pick = (lane8 == head + (row8 & 1)).astype(F32).astype(BF16)

        def chosen_pair(k):
            return chosen_rows([(me ^ k) * group, (me ^ (k + 1)) * group], group)

        def finish(out, sent):
            out[:group, :] = sent[:, :LANES].astype(BF16)
            query = sent[:, LANES:]
            out[group : group + half, :] = jnp.where(
                part < head, query[:half], pltpu.roll(query[half:], head, 1)
            ).astype(BF16)
            query = query.astype(BF16)
            spots = dot_nt(pick, query[:LANES])
            more = jnp.concatenate(
                [query[LANES:], jnp.zeros((2 * LANES - group, LANES), BF16)], axis=0
            )
            out[group + half :, :] = jnp.where(row8 < 2, spots, dot_nt(pick, more)).astype(BF16)

        ahead = chosen_pair(0)
        for k in range(0, space, 2):
            now, ahead = ahead, (chosen_pair(k + 2) if k + 2 < space else None)
            for n in range(2):
                finish(outs[k + n], now[n * group : (n + 1) * group])
    else:
        step = 384

        def permute(n, carry):
            start = pl.multiple_of(n * step, step)
            outs[0][pl.ds(start, step), :] = chosen_rows([start], step).astype(BF16)
            return carry

        lax.fori_loop(0, tok // step, permute, 0)


def nest_kernel(head, compact, *refs):
    if compact:
        count = len(refs) - 4
        chunks, (first_ref, last_ref, q_ref, got_ref) = refs[:count], refs[count:]
        group = got_ref.shape[0] // count
        half = group // 2
        rest = group - LANES
        part = iota((half, LANES), 1)
        line = iota((1, LANES), 1)
        spots, tails = [], []
        for k in range(count):
            query = chunks[k][group : group + half, :].astype(F32)
            near = jnp.where(part < head, query, 0.0).astype(BF16)
            far = jnp.where(part < head, pltpu.roll(query, head, 1), 0.0).astype(BF16)
            at, tail = k * LANES, count * LANES + k * rest
            got_ref[at : at + LANES, :LANES] = chunks[k][:LANES, :]
            got_ref[tail : tail + rest, :LANES] = chunks[k][LANES:group, :]
            got_ref[at : at + half, LANES:] = near
            got_ref[at + half : at + LANES, LANES:] = far[: LANES - half]
            got_ref[tail : tail + rest, LANES:] = far[LANES - half :]
            where = chunks[k][group + half :, :].astype(F32)
            spots.append(where[0:1] * float(BLOCK) + where[1:2])
            tails.append(where[2:3] * float(BLOCK) + where[3:4])
        for k in range(0, count, 2):
            spots.append(jnp.where(line < rest, tails[k], pltpu.roll(tails[k + 1], rest, 1)))
        slots = jnp.concatenate(spots, axis=1).astype(jnp.int32)
    else:
        got_ref, first_ref, last_ref, q_ref = refs
        lane, row = iota((8, LANES), 1), iota((8, LANES), 0)
        pick = (lane == row + head).astype(F32).astype(BF16)
        parts = dot_nt(pick, got_ref[:, LANES:])
        slots = (parts[0:1] * float(BLOCK) + parts[1:2]).astype(jnp.int32)
    tok = got_ref.shape[0]
    step = 384
    keep = iota((step, LANES), 1) < head
    edge = first_ref.shape[0]

    def nested_rows(start):
        chosen = (iota((step, tok), 0) + start == slots).astype(F32).astype(BF16)
        return dot(chosen, got_ref[...])

    ahead = nested_rows(0)
    for start in range(0, tok, step):
        nested, ahead = ahead, (nested_rows(start + step) if start + step < tok else None)
        target, at = (first_ref, start) if start < edge else (last_ref, start - edge)
        target[at : at + step, :] = nested[:, :LANES].astype(BF16)
        q_ref[start : start + step, :] = jnp.where(keep, nested[:, LANES:], 0.0).astype(BF16)


def bias_of(near_ref, region_blocks, bias_ref):
    near = near_ref[...]
    blocks, slots = near.shape
    all_blocks = region_blocks * lax.axis_size("space")
    at = near - lax.axis_index("space") * region_blocks
    at = jnp.where(at >= all_blocks // 2, at - all_blocks, at)
    at = jnp.where(at < -(all_blocks // 2), at + all_blocks, at)
    at = jnp.where(near >= 0, at + REACH, -1)
    lane = iota((blocks, LANES), 1)
    bias = jnp.full((blocks, LANES), -1e30, F32)
    for s in range(slots):
        bias = jnp.where(lane == at[:, s : s + 1], 0.0, bias)
    for j in range(region_blocks + 2 * REACH):
        bias_ref[:, j * BLOCK : (j + 1) * BLOCK] = jnp.broadcast_to(
            bias[:, j : j + 1], (blocks, BLOCK)
        )


def attend_tiles(query, keys, bias_ref, b, first):
    scores = dot_nt(query, keys)
    return [
        scores[:, n * BLOCK : (n + 1) * BLOCK]
        + bias_ref[b : b + 1, (first + n) * BLOCK : (first + n + 1) * BLOCK]
        for n in range(keys.shape[0] // BLOCK)
    ]


def largest(parts):
    return jnp.max(functools.reduce(jnp.maximum, parts), axis=1, keepdims=True)


def weigh(parts, top, keys):
    exps = [jnp.exp(part - top) for part in parts]
    total = jnp.sum(functools.reduce(jnp.add, exps), axis=1, keepdims=True)
    weights = jnp.concatenate([e.astype(BF16) for e in exps], axis=1)
    return dot(weights, keys), total


def local_kernel(near_ref, q_ref, first_ref, last_ref, acc_ref, top_ref, total_ref, bias_ref):
    region_blocks = q_ref.shape[0] // BLOCK
    edge = first_ref.shape[0] // BLOCK
    bias_of(near_ref, region_blocks, bias_ref)

    def keys_of(low, high):
        parts = []
        if low < edge:
            parts.append(first_ref[low * BLOCK : min(high, edge) * BLOCK, :])
        if high > edge:
            parts.append(last_ref[max(low - edge, 0) * BLOCK : (high - edge) * BLOCK, :])
        return parts[0] if len(parts) == 1 else jnp.concatenate(parts, axis=0)

    def score(b):
        low, high = max(0, b - REACH), min(region_blocks, b + REACH + 1)
        keys = keys_of(low, high)
        query = q_ref[b * BLOCK : (b + 1) * BLOCK, :]
        return attend_tiles(query, keys, bias_ref, b, low + REACH), keys

    ahead = score(0)
    for b in range(region_blocks):
        (parts, keys), ahead = ahead, (score(b + 1) if b + 1 < region_blocks else None)
        top = largest(parts)
        values, total = weigh(parts, top, keys)
        at = slice(b * BLOCK, (b + 1) * BLOCK)
        acc_ref[at, :] = values
        top_ref[at, :] = jnp.broadcast_to(top, (BLOCK, LANES))
        total_ref[at, :] = jnp.broadcast_to(total, (BLOCK, LANES))


def halo_kernel(head, mp, q_ref, before_ref, after_ref, acc_ref, top_ref, total_ref, bias_ref,
                out_ref):
    region_blocks = q_ref.shape[0] // BLOCK
    blocks = region_blocks // mp
    half = blocks * BLOCK // 2
    lane = iota((half, LANES), 1)

    def score(b):
        query = q_ref[b * BLOCK : (b + 1) * BLOCK, :]
        sides = []
        if b < REACH:
            sides.append((before_ref[b * BLOCK :, :], b))
        if b + REACH >= region_blocks:
            count = b + REACH + 1 - region_blocks
            sides.append((after_ref[: count * BLOCK, :], region_blocks + REACH))
        return sides, [attend_tiles(query, keys, bias_ref, b, first) for keys, first in sides]

    outputs = []
    queue = [score(b) for b in range(AHEAD)]
    for b in range(region_blocks):
        if b + AHEAD < region_blocks:
            queue.append(score(b + AHEAD))
        sides, scored = queue.pop(0)
        at = slice(b * BLOCK, (b + 1) * BLOCK)
        old = top_ref[at, :]
        top = old
        for parts in scored:
            top = jnp.maximum(top, largest(parts))
        keep = jnp.exp(old - top)
        values, total = acc_ref[at, :] * keep, total_ref[at, :] * keep
        for (keys, _), parts in zip(sides, scored):
            more, added = weigh(parts, top, keys)
            values, total = values + more, total + added
        outputs.append(values / total)
        if (b + 1) % blocks == 0:
            rows = jnp.concatenate(outputs, axis=0)
            outputs = []
            out_ref[shift_to(b // blocks)] = jnp.where(
                lane < head, pltpu.roll(rows[:half], head, 1), rows[half:]
            ).astype(BF16)


def shift_to(target):
    mp = lax.axis_size("mp")
    me = lax.axis_index("mp")
    return (me ^ target) if mp & (mp - 1) == 0 else lax.rem(target + mp - me, mp)


def source_of(shift):
    mp = lax.axis_size("mp")
    me = lax.axis_index("mp")
    return (me ^ shift) if mp & (mp - 1) == 0 else lax.rem(me + (mp - shift), mp)


def mix_kernel(shifts, head, *refs):
    mp = len(shifts)
    parts, w_ref, out_hbm, buf, out_buf, sems = refs[:mp], *refs[mp:]
    half = parts[0].shape[0]
    for shift, part in zip(shifts, parts):
        buf[source_of(shift)] = part[...]
    lane = iota((half, LANES), 1)
    upper, lower = [], []
    for pair in range(mp // 2):
        a = buf[2 * pair].astype(F32)
        b = buf[2 * pair + 1].astype(F32)
        upper.append(jnp.where(lane < head, a, pltpu.roll(b, head, 1)).astype(BF16))
        lower.append(jnp.where(lane < head, pltpu.roll(a, head, 1), b).astype(BF16))
    weights = w_ref[...]
    copies = []
    for n, rows in enumerate((upper, lower)):
        span = pl.ds(n * half, half)
        out_buf[span, :] = dot(jnp.concatenate(rows, axis=1), weights).astype(BF16)
        copies.append(
            pltpu.make_async_copy(out_buf.at[span, :], out_hbm.at[span, :], sems.at[n])
        )
        copies[-1].start()
    for copy in copies:
        copy.wait()


VMEM = pl.BlockSpec(memory_space=pltpu.VMEM)
SMEM = pl.BlockSpec(memory_space=pltpu.SMEM)
HBM = pl.BlockSpec(memory_space=pltpu.HBM)


def params(mib):
    return pltpu.CompilerParams(vmem_limit_bytes=mib << 20)


def per_device(tokens, norm_gain, w_qkv, w_out, head_scale, cycle_to_nested, neighbours):
    tok, width = tokens.shape
    space, mp = lax.axis_size("space"), lax.axis_size("mp")
    head = w_qkv.shape[2] // 3
    group = tok // space
    row_count = -(-tok // (8 * LANES)) * 8
    compact = space in (2, 4, 8) and group == LANES + LANES // 2
    chunk_rows = group + group // 2 + 8
    sent = pl.pallas_call(
        functools.partial(send_kernel, space, compact),
        out_shape=(jax.ShapeDtypeStruct((chunk_rows, LANES), BF16),) * space
        if compact
        else (jax.ShapeDtypeStruct((tok, TILE), BF16),),
        in_specs=[SMEM] + [HBM] * 4,
        out_specs=(VMEM,) * (space if compact else 1),
        scratch_shapes=[
            *([pltpu.VMEM((width // LANES, TILE, LANES), BF16)] * (2 * tok // TILE)),
            *([pltpu.VMEM((TILE, LANES), F32)] * (tok // TILE)),
            pltpu.VMEM((width // LANES, 3 * head, LANES), BF16),
            pltpu.VMEM((1, width), F32),
            pltpu.VMEM((row_count, LANES), jnp.int32),
            pltpu.VMEM((TILE, tok), BF16),
            pltpu.SemaphoreType.DMA((tok // TILE + 3,)),
        ],
        compiler_params=params(24),
        name="send",
    )(
        head_scale,
        *(
            pltpu.with_memory_space_constraint(x, pltpu.HBM)
            for x in (
                tokens,
                norm_gain.reshape(1, width),
                w_qkv.reshape(width, 3 * head).T,
                cycle_to_nested.reshape(tok // LANES, LANES),
            )
        ),
    )
    edge = REACH * BLOCK
    if compact:
        got = [sent[0]]
        for k in [7, 6, 4, 5, 2, 3, 1]:
            got.append(lax.ppermute(sent[k], "space", [(i, i ^ k) for i in range(space)]))
    else:
        got = [
            lax.all_to_all(
                sent[0].reshape(space, group, TILE), "space", 0, 0, tiled=True
            ).reshape(tok, TILE)
        ]
    first, last, query = pl.pallas_call(
        functools.partial(nest_kernel, head, compact),
        out_shape=(
            jax.ShapeDtypeStruct((edge, LANES), BF16),
            jax.ShapeDtypeStruct((tok - edge, LANES), BF16),
            jax.ShapeDtypeStruct((tok, LANES), BF16),
        ),
        in_specs=[VMEM] * len(got),
        out_specs=(VMEM,) * 3,
        scratch_shapes=[pltpu.VMEM((tok, TILE), BF16)] if compact else [],
        compiler_params=params(16),
        name="nest",
    )(*got)
    up = [(i, (i + 1) % space) for i in range(space)]
    down = [(j, i) for i, j in up]
    before = lax.ppermute(last[last.shape[0] - edge :], "space", up)
    after = lax.ppermute(first, "space", down)
    region_blocks = tok // BLOCK
    blocks = region_blocks // mp
    state = pl.pallas_call(
        local_kernel,
        out_shape=[jax.ShapeDtypeStruct((tok, LANES), F32)] * 3
        + [jax.ShapeDtypeStruct((region_blocks, (region_blocks + 2 * REACH) * BLOCK), F32)],
        in_specs=[VMEM] * 4,
        out_specs=[VMEM] * 4,
        compiler_params=params(24),
        name="local",
    )(neighbours, query, first, last)
    order = list(range(mp))
    parts = pl.pallas_call(
        functools.partial(halo_kernel, head, mp),
        out_shape=jax.ShapeDtypeStruct((mp, blocks * BLOCK // 2, LANES), BF16),
        in_specs=[VMEM] * 7,
        out_specs=VMEM,
        compiler_params=params(24),
        name="halo",
    )(query, before, after, *state)
    received = [parts[0]]
    xor = mp & (mp - 1) == 0
    for k in order[1:]:
        route = [(i, (i ^ k) if xor else (i + k) % mp) for i in range(mp)]
        received.append(lax.ppermute(parts[k], "mp", route))
    out_shape = (tok // mp, w_out.shape[1])
    return pl.pallas_call(
        functools.partial(mix_kernel, order, head),
        out_shape=jax.ShapeDtypeStruct(out_shape, BF16),
        in_specs=[VMEM] * (mp + 1),
        out_specs=HBM,
        scratch_shapes=[
            pltpu.VMEM((mp, blocks * BLOCK // 2, LANES), BF16),
            pltpu.VMEM(out_shape, BF16),
            pltpu.SemaphoreType.DMA((4,)),
        ],
        compiler_params=params(16),
        name="mix",
    )(*received, w_out)


def solution(mesh):
    placed = (
        P("space", None),
        P(),
        P(None, "mp", None),
        P(),
        P("mp"),
        P("space"),
        P("space", None),
    )
    return jax.shard_map(
        per_device, mesh=mesh, in_specs=placed, out_specs=P(("space", "mp"), None), check_vma=False
    )
```

```python
import functools

import jax
import jax.numpy as jnp
from jax import lax
from jax.experimental import pallas as pl
from jax.experimental.pallas import tpu as pltpu
from jax.sharding import PartitionSpec as P

BLOCK = 128
REACH = 6
LANES = 128
TILE = 256
AHEAD = 3
F32 = jnp.float32
BF16 = jnp.bfloat16


def dot(a, b):
    return jnp.dot(a, b, preferred_element_type=F32)


def dot_nt(a, b):
    return lax.dot_general(a, b, (((1,), (1,)), ((), ())), preferred_element_type=F32)


def iota(shape, dim):
    return lax.broadcasted_iota(jnp.int32, shape, dim)


def send_kernel(space, compact, scale_ref, tokens_hbm, gain_hbm, w_hbm, slots_hbm, *refs):
    tok, width = tokens_hbm.shape
    tiles = tok // TILE
    outs, bufs = refs[: -5 - 3 * tiles], refs[-5 - 3 * tiles : -5]
    tok_bufs, norm_bufs, factor_bufs = (bufs[n * tiles : (n + 1) * tiles] for n in range(3))
    w_buf, gain_buf, slots_buf, packed_buf, sems = refs[-5:]
    group = tok // space
    head = w_hbm.shape[0] // 3
    slot_rows = slots_hbm.shape[0]
    rows = slots_buf.shape[0]
    small = [
        pltpu.make_async_copy(slots_hbm, slots_buf.at[pl.ds(0, slot_rows), :], sems.at[tiles + 1]),
        pltpu.make_async_copy(gain_hbm, gain_buf, sems.at[tiles + 2]),
    ]
    spans = [(c, slice(c * LANES, (c + 1) * LANES)) for c in range(width // LANES)]

    def fetch(i):
        return [
            pltpu.make_async_copy(
                tokens_hbm.at[pl.ds(i * TILE, TILE), pl.ds(c * LANES, LANES)],
                tok_bufs[i].at[c],
                sems.at[i],
            )
            for c, _ in spans
        ]

    copies = [fetch(i) for i in range(tiles)]
    weight_copies = [
        pltpu.make_async_copy(
            w_hbm.at[:, pl.ds(c * LANES, LANES)],
            w_buf.at[c],
            sems.at[tiles],
        )
        for c, _ in spans
    ]
    for copy in small + copies[0] + weight_copies + sum(copies[1:], []):
        copy.start()

    small[0].wait()
    slots = jnp.where(iota((rows, LANES), 0) < slot_rows, slots_buf[...], -1)
    masks = [((slots >= d * tok) & (slots < (d + 1) * tok)) for d in range(space)]
    ones = [m.astype(F32) for m in masks]
    stacked = jnp.concatenate(ones, axis=0).astype(BF16)
    total_rows = rows * space
    earlier = (iota((LANES, LANES), 0) < iota((LANES, LANES), 1)).astype(F32).astype(BF16)
    in_row = dot(stacked, earlier)
    row_total = dot(stacked, jnp.ones((LANES, LANES), BF16)).astype(BF16)
    left, right = iota((total_rows, total_rows), 0), iota((total_rows, total_rows), 1)
    above = ((left // rows == right // rows) & (right < left)).astype(F32).astype(BF16)
    rank = in_row + dot(above, row_total)
    pos = jnp.full((rows, LANES), -1.0, F32)
    place = slots
    for d in range(space):
        pos = jnp.where(masks[d], rank[d * rows : (d + 1) * rows] + float(d * group), pos)
        place = jnp.where(masks[d], slots - d * tok, place)
    slots_buf[...] = pos.astype(jnp.int32)
    high = (place >> 7).astype(F32)
    low = (place & 127).astype(F32)
    small[1].wait()
    gain = gain_buf[...]
    scale = scale_ref[0]
    piece = 16
    row16 = iota((16, LANES), 0)

    zero = jnp.minimum(lax.axis_index("space"), 0)

    def measure(i):
        for start in range(0, TILE, piece):
            at = slice(start, start + piece)
            squares = []
            for c, _ in spans:
                values = tok_bufs[i][c, at, :].astype(F32)
                squares.append(values * values)
            while len(squares) > 1:
                squares = [x + y for x, y in zip(squares[::2], squares[1::2])]
            mean_square = jnp.sum(squares[0], axis=1, keepdims=True) / width
            factor_bufs[i][at, :] = jnp.broadcast_to(
                lax.rsqrt(mean_square + 1e-05), (piece, LANES)
            )

    def normalize(i):
        for start in range(0, TILE, piece):
            at = slice(start, start + piece)
            again = pl.ds(pl.multiple_of(zero + start, piece), piece)
            factor = factor_bufs[i][at, :]
            for c, span in spans:
                norm_bufs[i][c, at, :] = (
                    tok_bufs[i][c, again, :].astype(F32) * factor * gain[:, span]
                ).astype(BF16)

    def project(i):
        projected = dot_nt(
            jnp.concatenate([w_buf[c] for c, _ in spans], axis=1),
            jnp.concatenate([norm_bufs[i][c] for c, _ in spans], axis=1),
        )
        at = slice(i * TILE, (i + 1) * TILE)
        query, key = projected[:head], projected[head : 2 * head]
        query = query * (
            scale * lax.rsqrt(jnp.sum(query * query, axis=0, keepdims=True) + 1e-06)
        )
        key = key * lax.rsqrt(jnp.sum(key * key, axis=0, keepdims=True) + 1e-06)
        packed_buf[:head, at] = key.astype(BF16)
        packed_buf[head : 2 * head, at] = projected[2 * head :].astype(BF16)
        packed_buf[2 * head : 3 * head, at] = query.astype(BF16)

    for r in range(tok // LANES):
        packed_buf[3 * head : 3 * head + 16, r * LANES : (r + 1) * LANES] = jnp.where(
            row16 == 0,
            high[r : r + 1],
            jnp.where(row16 == 1, low[r : r + 1], 0.0),
        ).astype(BF16)
    packed_buf[3 * head + 16 :, :] = jnp.zeros((TILE - 3 * head - 16, tok), BF16)
    for i in range(tiles):
        pltpu.make_async_copy(tok_bufs[i], tok_bufs[i], sems.at[i]).wait()
        if i == 1:
            pltpu.make_async_copy(w_buf, w_buf, sems.at[tiles]).wait()
        if i:
            project(i - 1)
        measure(i)
        normalize(i)
    project(tiles - 1)

    def chosen_rows(starts, count):
        wanted = jnp.concatenate([iota((count, LANES), 0) + start for start in starts], axis=0)
        chosen = jnp.concatenate(
            [
                (wanted == slots_buf[r : r + 1, :]).astype(F32).astype(BF16)
                for r in range(tok // LANES)
            ],
            axis=1,
        )
        return dot_nt(chosen, packed_buf[...])

    if compact:
        me = lax.axis_index("space")
        half = group // 2
        part = iota((half, LANES), 1)
        row8, lane8 = iota((8, LANES), 0), iota((8, LANES), 1)
        pick = (lane8 == head + (row8 & 1)).astype(F32).astype(BF16)

        def chosen_pair(k):
            return chosen_rows([(me ^ k) * group, (me ^ (k + 1)) * group], group)

        def finish(out, sent):
            out[:group, :] = sent[:, :LANES].astype(BF16)
            query = sent[:, LANES:]
            out[group : group + half, :] = jnp.where(
                part < head, query[:half], pltpu.roll(query[half:], head, 1)
            ).astype(BF16)
            query = query.astype(BF16)
            spots = dot_nt(pick, query[:LANES])
            more = jnp.concatenate(
                [query[LANES:], jnp.zeros((2 * LANES - group, LANES), BF16)], axis=0
            )
            out[group + half :, :] = jnp.where(row8 < 2, spots, dot_nt(pick, more)).astype(BF16)

        ahead = chosen_pair(0)
        for k in range(0, space, 2):
            now, ahead = ahead, (chosen_pair(k + 2) if k + 2 < space else None)
            for n in range(2):
                finish(outs[k + n], now[n * group : (n + 1) * group])
    else:
        step = 384

        def permute(n, carry):
            start = pl.multiple_of(n * step, step)
            outs[0][pl.ds(start, step), :] = chosen_rows([start], step).astype(BF16)
            return carry

        lax.fori_loop(0, tok // step, permute, 0)


def nest_kernel(head, compact, *refs):
    if compact:
        count = len(refs) - 4
        chunks, (first_ref, last_ref, q_ref, got_ref) = refs[:count], refs[count:]
        group = got_ref.shape[0] // count
        half = group // 2
        rest = group - LANES
        part = iota((half, LANES), 1)
        line = iota((1, LANES), 1)
        spots, tails = [], []
        for k in range(count):
            query = chunks[k][group : group + half, :].astype(F32)
            near = jnp.where(part < head, query, 0.0).astype(BF16)
            far = jnp.where(part < head, pltpu.roll(query, head, 1), 0.0).astype(BF16)
            at, tail = k * LANES, count * LANES + k * rest
            got_ref[at : at + LANES, :LANES] = chunks[k][:LANES, :]
            got_ref[tail : tail + rest, :LANES] = chunks[k][LANES:group, :]
            got_ref[at : at + half, LANES:] = near
            got_ref[at + half : at + LANES, LANES:] = far[: LANES - half]
            got_ref[tail : tail + rest, LANES:] = far[LANES - half :]
            where = chunks[k][group + half :, :].astype(F32)
            spots.append(where[0:1] * float(BLOCK) + where[1:2])
            tails.append(where[2:3] * float(BLOCK) + where[3:4])
        for k in range(0, count, 2):
            spots.append(jnp.where(line < rest, tails[k], pltpu.roll(tails[k + 1], rest, 1)))
        slots = jnp.concatenate(spots, axis=1).astype(jnp.int32)
    else:
        got_ref, first_ref, last_ref, q_ref = refs
        lane, row = iota((8, LANES), 1), iota((8, LANES), 0)
        pick = (lane == row + head).astype(F32).astype(BF16)
        parts = dot_nt(pick, got_ref[:, LANES:])
        slots = (parts[0:1] * float(BLOCK) + parts[1:2]).astype(jnp.int32)
    tok = got_ref.shape[0]
    step = 384
    keep = iota((step, LANES), 1) < head
    edge = first_ref.shape[0]

    def nested_rows(start):
        chosen = (iota((step, tok), 0) + start == slots).astype(F32).astype(BF16)
        return dot(chosen, got_ref[...])

    ahead = nested_rows(0)
    for start in range(0, tok, step):
        nested, ahead = ahead, (nested_rows(start + step) if start + step < tok else None)
        target, at = (first_ref, start) if start < edge else (last_ref, start - edge)
        target[at : at + step, :] = nested[:, :LANES].astype(BF16)
        q_ref[start : start + step, :] = jnp.where(keep, nested[:, LANES:], 0.0).astype(BF16)


def bias_of(near_ref, region_blocks, bias_ref):
    near = near_ref[...]
    blocks, slots = near.shape
    all_blocks = region_blocks * lax.axis_size("space")
    at = near - lax.axis_index("space") * region_blocks
    at = jnp.where(at >= all_blocks // 2, at - all_blocks, at)
    at = jnp.where(at < -(all_blocks // 2), at + all_blocks, at)
    at = jnp.where(near >= 0, at + REACH, -1)
    lane = iota((blocks, LANES), 1)
    bias = jnp.full((blocks, LANES), -1e30, F32)
    for s in range(slots):
        bias = jnp.where(lane == at[:, s : s + 1], 0.0, bias)
    for j in range(region_blocks + 2 * REACH):
        bias_ref[:, j * BLOCK : (j + 1) * BLOCK] = jnp.broadcast_to(
            bias[:, j : j + 1], (blocks, BLOCK)
        )


def attend_tiles(query, keys, bias_ref, b, first):
    scores = dot_nt(query, keys)
    return [
        scores[:, n * BLOCK : (n + 1) * BLOCK]
        + bias_ref[b : b + 1, (first + n) * BLOCK : (first + n + 1) * BLOCK]
        for n in range(keys.shape[0] // BLOCK)
    ]


def largest(parts):
    return jnp.max(functools.reduce(jnp.maximum, parts), axis=1, keepdims=True)


def weigh(parts, top, keys):
    exps = [jnp.exp(part - top) for part in parts]
    total = jnp.sum(functools.reduce(jnp.add, exps), axis=1, keepdims=True)
    weights = jnp.concatenate([e.astype(BF16) for e in exps], axis=1)
    return dot(weights, keys), total


def local_kernel(near_ref, q_ref, first_ref, last_ref, acc_ref, top_ref, total_ref, bias_ref):
    region_blocks = q_ref.shape[0] // BLOCK
    edge = first_ref.shape[0] // BLOCK
    bias_of(near_ref, region_blocks, bias_ref)

    def keys_of(low, high):
        parts = []
        if low < edge:
            parts.append(first_ref[low * BLOCK : min(high, edge) * BLOCK, :])
        if high > edge:
            parts.append(last_ref[max(low - edge, 0) * BLOCK : (high - edge) * BLOCK, :])
        return parts[0] if len(parts) == 1 else jnp.concatenate(parts, axis=0)

    def score(b):
        low, high = max(0, b - REACH), min(region_blocks, b + REACH + 1)
        keys = keys_of(low, high)
        query = q_ref[b * BLOCK : (b + 1) * BLOCK, :]
        return attend_tiles(query, keys, bias_ref, b, low + REACH), keys

    ahead = score(0)
    for b in range(region_blocks):
        (parts, keys), ahead = ahead, (score(b + 1) if b + 1 < region_blocks else None)
        top = largest(parts)
        values, total = weigh(parts, top, keys)
        at = slice(b * BLOCK, (b + 1) * BLOCK)
        acc_ref[at, :] = values
        top_ref[at, :] = jnp.broadcast_to(top, (BLOCK, LANES))
        total_ref[at, :] = jnp.broadcast_to(total, (BLOCK, LANES))


def halo_kernel(head, mp, q_ref, before_ref, after_ref, acc_ref, top_ref, total_ref, bias_ref,
                out_ref):
    region_blocks = q_ref.shape[0] // BLOCK
    blocks = region_blocks // mp
    half = blocks * BLOCK // 2
    lane = iota((half, LANES), 1)

    def score(b):
        query = q_ref[b * BLOCK : (b + 1) * BLOCK, :]
        sides = []
        if b < REACH:
            sides.append((before_ref[b * BLOCK :, :], b))
        if b + REACH >= region_blocks:
            count = b + REACH + 1 - region_blocks
            sides.append((after_ref[: count * BLOCK, :], region_blocks + REACH))
        return sides, [attend_tiles(query, keys, bias_ref, b, first) for keys, first in sides]

    outputs = []
    queue = [score(b) for b in range(AHEAD)]
    for b in range(region_blocks):
        if b + AHEAD < region_blocks:
            queue.append(score(b + AHEAD))
        sides, scored = queue.pop(0)
        at = slice(b * BLOCK, (b + 1) * BLOCK)
        old = top_ref[at, :]
        top = old
        for parts in scored:
            top = jnp.maximum(top, largest(parts))
        keep = jnp.exp(old - top)
        values, total = acc_ref[at, :] * keep, total_ref[at, :] * keep
        for (keys, _), parts in zip(sides, scored):
            more, added = weigh(parts, top, keys)
            values, total = values + more, total + added
        outputs.append(values / total)
        if (b + 1) % blocks == 0:
            rows = jnp.concatenate(outputs, axis=0)
            outputs = []
            out_ref[shift_to(b // blocks)] = jnp.where(
                lane < head, pltpu.roll(rows[:half], head, 1), rows[half:]
            ).astype(BF16)


def shift_to(target):
    mp = lax.axis_size("mp")
    me = lax.axis_index("mp")
    return (me ^ target) if mp & (mp - 1) == 0 else lax.rem(target + mp - me, mp)


def source_of(shift):
    mp = lax.axis_size("mp")
    me = lax.axis_index("mp")
    return (me ^ shift) if mp & (mp - 1) == 0 else lax.rem(me + (mp - shift), mp)


def mix_kernel(shifts, head, *refs):
    mp = len(shifts)
    parts, w_ref, out_hbm, buf, out_buf, sems = refs[:mp], *refs[mp:]
    half = parts[0].shape[0]
    for shift, part in zip(shifts, parts):
        buf[source_of(shift)] = part[...]
    lane = iota((half, LANES), 1)
    upper, lower = [], []
    for pair in range(mp // 2):
        a = buf[2 * pair].astype(F32)
        b = buf[2 * pair + 1].astype(F32)
        upper.append(jnp.where(lane < head, a, pltpu.roll(b, head, 1)).astype(BF16))
        lower.append(jnp.where(lane < head, pltpu.roll(a, head, 1), b).astype(BF16))
    weights = w_ref[...]
    copies = []
    mixed = [dot(jnp.concatenate(rows, axis=1), weights) for rows in (upper, lower)]
    for n, rows in enumerate(mixed):
        span = pl.ds(n * half, half)
        out_buf[span, :] = rows.astype(BF16)
        copies.append(
            pltpu.make_async_copy(out_buf.at[span, :], out_hbm.at[span, :], sems.at[n])
        )
        copies[-1].start()
    for copy in copies:
        copy.wait()


VMEM = pl.BlockSpec(memory_space=pltpu.VMEM)
SMEM = pl.BlockSpec(memory_space=pltpu.SMEM)
HBM = pl.BlockSpec(memory_space=pltpu.HBM)


def params(mib):
    return pltpu.CompilerParams(vmem_limit_bytes=mib << 20)


def per_device(tokens, norm_gain, w_qkv, w_out, head_scale, cycle_to_nested, neighbours):
    tok, width = tokens.shape
    space, mp = lax.axis_size("space"), lax.axis_size("mp")
    head = w_qkv.shape[2] // 3
    group = tok // space
    row_count = -(-tok // (8 * LANES)) * 8
    compact = space in (2, 4, 8) and group == LANES + LANES // 2
    chunk_rows = group + group // 2 + 8
    sent = pl.pallas_call(
        functools.partial(send_kernel, space, compact),
        out_shape=(jax.ShapeDtypeStruct((chunk_rows, LANES), BF16),) * space
        if compact
        else (jax.ShapeDtypeStruct((tok, TILE), BF16),),
        in_specs=[SMEM] + [HBM] * 4,
        out_specs=(VMEM,) * (space if compact else 1),
        scratch_shapes=[
            *([pltpu.VMEM((width // LANES, TILE, LANES), BF16)] * (2 * tok // TILE)),
            *([pltpu.VMEM((TILE, LANES), F32)] * (tok // TILE)),
            pltpu.VMEM((width // LANES, 3 * head, LANES), BF16),
            pltpu.VMEM((1, width), F32),
            pltpu.VMEM((row_count, LANES), jnp.int32),
            pltpu.VMEM((TILE, tok), BF16),
            pltpu.SemaphoreType.DMA((tok // TILE + 3,)),
        ],
        compiler_params=params(24),
        name="send",
    )(
        head_scale,
        *(
            pltpu.with_memory_space_constraint(x, pltpu.HBM)
            for x in (
                tokens,
                norm_gain.reshape(1, width),
                w_qkv.reshape(width, 3 * head).T,
                cycle_to_nested.reshape(tok // LANES, LANES),
            )
        ),
    )
    edge = REACH * BLOCK
    if compact:
        got = [sent[0]]
        for k in [7, 6, 4, 5, 2, 3, 1]:
            got.append(lax.ppermute(sent[k], "space", [(i, i ^ k) for i in range(space)]))
    else:
        got = [
            lax.all_to_all(
                sent[0].reshape(space, group, TILE), "space", 0, 0, tiled=True
            ).reshape(tok, TILE)
        ]
    first, last, query = pl.pallas_call(
        functools.partial(nest_kernel, head, compact),
        out_shape=(
            jax.ShapeDtypeStruct((edge, LANES), BF16),
            jax.ShapeDtypeStruct((tok - edge, LANES), BF16),
            jax.ShapeDtypeStruct((tok, LANES), BF16),
        ),
        in_specs=[VMEM] * len(got),
        out_specs=(VMEM,) * 3,
        scratch_shapes=[pltpu.VMEM((tok, TILE), BF16)] if compact else [],
        compiler_params=params(16),
        name="nest",
    )(*got)
    up = [(i, (i + 1) % space) for i in range(space)]
    down = [(j, i) for i, j in up]
    before = lax.ppermute(last[last.shape[0] - edge :], "space", up)
    after = lax.ppermute(first, "space", down)
    region_blocks = tok // BLOCK
    blocks = region_blocks // mp
    state = pl.pallas_call(
        local_kernel,
        out_shape=[jax.ShapeDtypeStruct((tok, LANES), F32)] * 3
        + [jax.ShapeDtypeStruct((region_blocks, (region_blocks + 2 * REACH) * BLOCK), F32)],
        in_specs=[VMEM] * 4,
        out_specs=[VMEM] * 4,
        compiler_params=params(24),
        name="local",
    )(neighbours, query, first, last)
    order = list(range(mp))
    parts = pl.pallas_call(
        functools.partial(halo_kernel, head, mp),
        out_shape=jax.ShapeDtypeStruct((mp, blocks * BLOCK // 2, LANES), BF16),
        in_specs=[VMEM] * 7,
        out_specs=VMEM,
        compiler_params=params(24),
        name="halo",
    )(query, before, after, *state)
    received = [parts[0]]
    xor = mp & (mp - 1) == 0
    for k in order[1:]:
        route = [(i, (i ^ k) if xor else (i + k) % mp) for i in range(mp)]
        received.append(lax.ppermute(parts[k], "mp", route))
    out_shape = (tok // mp, w_out.shape[1])
    return pl.pallas_call(
        functools.partial(mix_kernel, order, head),
        out_shape=jax.ShapeDtypeStruct(out_shape, BF16),
        in_specs=[VMEM] * (mp + 1),
        out_specs=HBM,
        scratch_shapes=[
            pltpu.VMEM((mp, blocks * BLOCK // 2, LANES), BF16),
            pltpu.VMEM(out_shape, BF16),
            pltpu.SemaphoreType.DMA((4,)),
        ],
        compiler_params=params(16),
        name="mix",
    )(*received, w_out)


def solution(mesh):
    placed = (
        P("space", None),
        P(),
        P(None, "mp", None),
        P(),
        P("mp"),
        P("space"),
        P("space", None),
    )
    return jax.shard_map(
        per_device, mesh=mesh, in_specs=placed, out_specs=P(("space", "mp"), None), check_vma=False
    )
```
